32 devices in a mesh: clip: 4 (over y, x), tile: 8 (over z, core).
Axes of the slice: x: 2, y: 2, z: 4, core: 2. Of those that a mesh axis runs over, the one named last changes fastest.
Arguments:
- clip_features: bfloat16 [4, 9, 24, 32, 128], P('clip', None, 'tile'), may hold values from -6 to 6
- upstream: bfloat16 [4, 9, 24, 32, 128], P('clip', None, 'tile'), may hold values from -3 to 3
- weight: bfloat16 [27, 128, 128], replicated, may hold values from -0.109375 to 0.109375
- conv_bias: float32 [128], replicated, may hold values from -2 to 2
Outputs:
- grad_weight: float32 [3456, 128], P('tile')
- grad_bias: float32 [128], replicated
- penalty: float32 [], replicated
The draws below stay inside these ranges and needn't reach their ends.
All inputs are finite; a program needn't handle non-finite values.
Results may differ from the reference program's by a relative error of at most 0.002.
Values may be sent and summed in bfloat16 or wider, within the bound.
A program may use at most 64 MiB of HBM per device.

```python
import jax
import jax.numpy as jnp
from jax import lax

C = 128
TAPS = 27
FRAMES = 9
HEIGHT = 32
CLIPS = 4
WIDTH = 24
CELLS = 27648


def block_scale(key, shape, cuts, smallest, largest):
    level = 1.0
    for axis_at, shards_of in cuts:
        steps = jax.random.uniform(jax.random.fold_in(jax.random.fold_in(key, 6), axis_at), (shards_of,), jnp.float32, smallest / len(cuts), largest / len(cuts))
        level = level * jnp.repeat(jnp.exp(steps), shape[axis_at] // shards_of).reshape((-1,) + (1,) * (len(shape) - 1 - axis_at))
    return level


def bell_draw(rng, dims, deviation, limit, shards=(), dtype=jnp.bfloat16):
    gain = block_scale(rng, dims, shards, -0.22, 0.18) if shards else 1.0
    drawn = jax.random.normal(rng, dims, jnp.float32) * deviation * gain
    return jnp.minimum(jnp.maximum(drawn, -limit), limit).astype(dtype)


def setup_inputs(seed: int = 0) -> dict:
    splits = jax.random.split(jax.random.key(seed), 5)
    clip_features = bell_draw(splits[0], (CLIPS, FRAMES, WIDTH, HEIGHT, C), 1.0, 6.0, ((0, 4), (2, 8)))
    upstream = bell_draw(splits[1], (CLIPS, FRAMES, WIDTH, HEIGHT, C), 0.5, 3.0, ((0, 4), (2, 8)))
    weight = bell_draw(splits[2], (TAPS, C, C), (TAPS * C) ** -0.5, 0.109375)
    conv_bias = bell_draw(splits[3], (C,), 0.5, 2.0, (), jnp.float32)
    return {"clip_features": clip_features, "upstream": upstream, "weight": weight, "conv_bias": conv_bias}


r1_weight = 10.0


def slope_of(value):
    return 0.2 + 0.8 * jax.nn.sigmoid(value)


def bend_of(value):
    sigma = jax.nn.sigmoid(value)
    return 0.8 * sigma * (1.0 - sigma)


def pad_cells(field):
    return jnp.pad(field, ((1, 1), (1, 1), (1, 1), (0, 0)))


def conv_clip(field, weight, flipped):
    frames, columns, row_count, channels = field.shape
    padded = pad_cells(field)
    summed = jnp.zeros((frames * columns * row_count, weight.shape[2]), jnp.float32)
    for tap_f in range(3):
        for tap_w in range(3):
            for tap_h in range(3):
                index = 9 * tap_f + 3 * tap_w + tap_h
                if flipped:
                    piece = padded[2 - tap_f:2 - tap_f + frames, 2 - tap_w:2 - tap_w + columns, 2 - tap_h:2 - tap_h + row_count, :]
                    kernel = weight[index].T
                else:
                    piece = padded[tap_f:tap_f + frames, tap_w:tap_w + columns, tap_h:tap_h + row_count, :]
                    kernel = weight[index]
                summed = summed + jnp.dot(piece.reshape(-1, channels), kernel, preferred_element_type=jnp.float32)
    return summed.reshape(frames, columns, row_count, -1)


def wgrad_clip(field, gradients):
    frames, columns, row_count, channels = field.shape
    padded = pad_cells(field)
    flat_grads = gradients.reshape(-1, gradients.shape[-1])
    partials = []
    for tap_f in range(3):
        for tap_w in range(3):
            for tap_h in range(3):
                piece = padded[tap_f:tap_f + frames, tap_w:tap_w + columns, tap_h:tap_h + row_count, :]
                partials.append(lax.dot_general(piece.reshape(-1, channels), flat_grads, (((0,), (0,)), ((), ())), preferred_element_type=jnp.float32))
    return jnp.concatenate(partials, axis=0)


def reference(clip_features, upstream, weight, conv_bias):
    factor = r1_weight / CELLS

    def per_clip(clip_pair):
        features, upstream_clip = clip_pair
        upstream_f = upstream_clip.astype(jnp.float32)
        hidden = conv_clip(features, weight, False) + conv_bias
        grad_h = (upstream_f * slope_of(hidden)).astype(jnp.bfloat16)
        grad_x = conv_clip(grad_h, weight, True)
        squares = jnp.sum(grad_x * grad_x)
        grad_xb = grad_x.astype(jnp.bfloat16)
        back_conv = conv_clip(grad_xb, weight, False)
        curvature = (back_conv * upstream_f * bend_of(hidden)).astype(jnp.bfloat16)
        weight_terms = wgrad_clip(grad_xb, grad_h) + wgrad_clip(features, curvature)
        bias_terms = jnp.sum(curvature.astype(jnp.float32), axis=(0, 1, 2))
        return weight_terms, bias_terms, squares

    weight_terms, bias_terms, squares = lax.map(per_clip, (clip_features, upstream))
    grad_weight = factor * jnp.sum(weight_terms, axis=0)
    grad_bias = factor * jnp.sum(bias_terms, axis=0)
    penalty = 0.5 * factor * jnp.sum(squares)
    return grad_weight, grad_bias, penalty
```

```python
import functools

import jax
import jax.numpy as jnp
from jax import lax
from jax.experimental import pallas as pl
from jax.experimental.pallas import tpu as pltpu
from jax.sharding import PartitionSpec as P

r1_weight = 10.0
MESH = pl.DeviceIdType.MESH
BF16 = jnp.bfloat16
F32 = jnp.float32


def kernel(geo, x_hbm, up_hbm, w_hbm, bias_hbm, out_ref, *rest):
    scatter = geo[8]
    if scatter:
        bias_ref_out, pen_ref, *scratch = rest
    else:
        stat_ref, *scratch = rest
    (clips, tiles, frames, cols, rows, ch, block, piece, scatter, factor) = geo
    (bias_ref, bias_sem, xb, upb, wv, wt, x3, h3, g3, xt, gt, ghp, cvp, sig, hs, hr, gs, gr, st,
     load_sem, up_sem, w_sem, hx_send, hx_recv, hh_send, hh_recv, hg_send, hg_recv) = scratch[:28]
    k = lax.axis_index("clip")
    t = lax.axis_index("tile")
    cells = frames * rows
    wide = 3 * ch
    deep = x3.shape[1]
    lanes = deep * rows
    has_left = t > 0
    has_right = t < tiles - 1

    peers = [(0, dt) for dt in range(1, tiles)] + [(dk, 0) for dk in range(1, clips)]
    barrier = pltpu.get_barrier_semaphore()
    if scatter:
        for dk, dt in peers:
            pl.semaphore_signal(
                barrier, inc=1,
                device_id=(lax.rem(k + dk, clips), lax.rem(t + dt, tiles)), device_id_type=MESH,
            )
    else:
        for step in (1, tiles - 1):
            pl.semaphore_signal(
                barrier, inc=1, device_id=(k, lax.rem(t + step, tiles)), device_id_type=MESH
            )

    x_loads = [pltpu.make_async_copy(x_hbm.at[:, w], xb.at[w + 1], load_sem.at[w]) for w in range(cols)]
    for copy in x_loads:
        copy.start()
    w_loads = [
        pltpu.make_async_copy(
            w_hbm.at[3 * a + b], wv.at[wide * b:wide * (b + 1), a * ch:(a + 1) * ch], w_sem.at[3 * a + b]
        )
        for a in range(3)
        for b in range(3)
    ]
    for copy in w_loads:
        copy.start()
    up_loads = [pltpu.make_async_copy(up_hbm.at[:, w], upb.at[w], up_sem.at[w]) for w in range(cols)]
    for copy in up_loads:
        copy.start()
    bias_load = pltpu.make_async_copy(bias_hbm, bias_ref, bias_sem)
    bias_load.start()

    def swap(sources, targets, send_sem, recv_sem):
        to_left = pltpu.make_async_remote_copy(
            src_ref=sources[0], dst_ref=targets[1], send_sem=send_sem.at[0], recv_sem=recv_sem.at[1],
            device_id=(k, jnp.maximum(t - 1, 0)), device_id_type=MESH,
        )
        to_right = pltpu.make_async_remote_copy(
            src_ref=sources[1], dst_ref=targets[0], send_sem=send_sem.at[1], recv_sem=recv_sem.at[0],
            device_id=(k, jnp.minimum(t + 1, tiles - 1)), device_id_type=MESH,
        )
        return to_left, to_right

    def start(copies, side):
        @pl.when(has_left if side == 0 else has_right)
        def _():
            copies[side].start()

    def finish_recv(copies, side):
        @pl.when(has_left if side == 0 else has_right)
        def _():
            copies[1 - side].wait_recv()

    def finish_send(copies):
        for side in range(2):
            @pl.when(has_left if side == 0 else has_right)
            def _():
                copies[side].wait_send()

    x_swap = swap((xb.at[1], xb.at[cols]), (xb.at[0], xb.at[cols + 1]), hx_send, hx_recv)
    h_swap = swap((hs.at[0], hs.at[1]), (hr.at[0], hr.at[1]), hh_send, hh_recv)
    g_swap = swap((gs.at[0], gs.at[1]), (gr.at[0], gr.at[1]), hg_send, hg_recv)

    zero_wide = jnp.zeros((rows, wide), BF16)
    for field in (x3, g3):
        for w in range(cols + 2):
            for f in range(frames, deep):
                field[w, f] = zero_wide
    zero_thin = jnp.zeros((rows, ch), BF16)
    for field in (ghp, cvp):
        for w in range(cols):
            for f in [0] + list(range(frames + 1, field.shape[1])):
                field[w, f] = zero_thin
    zero_col = jnp.zeros((frames, rows, ch), BF16)

    @pl.when(jnp.logical_not(has_left))
    def _():
        xb[0] = zero_col
        hr[0] = zero_col
        gr[0] = zero_col

    @pl.when(jnp.logical_not(has_right))
    def _():
        xb[cols + 1] = zero_col
        hr[1] = zero_col
        gr[1] = zero_col

    row_at = lax.rem(lax.broadcasted_iota(jnp.int32, (cells, ch), 0), rows)
    first_row = row_at == 0
    last_row = row_at == rows - 1

    def widen(value, field, w):
        before = jnp.where(first_row, 0.0, pltpu.roll(value, 1, 0)).astype(BF16)
        after = jnp.where(last_row, 0.0, pltpu.roll(value, cells - 1, 0)).astype(BF16)
        shape = (frames, rows, ch)
        field[w, 0:frames, :, 0:ch] = before.reshape(shape)
        field[w, 0:frames, :, ch:2 * ch] = value.astype(BF16).reshape(shape)
        field[w, 0:frames, :, 2 * ch:] = after.reshape(shape)

    def flip(field, w, target):
        target[:, w * lanes:(w + 1) * lanes] = field[w].reshape(lanes, wide).T

    def conv(field, weights, w):
        left = jnp.concatenate(
            [field[w + b, 0:frames].reshape(cells, wide) for b in range(3)], axis=1
        )
        taps = jnp.dot(left, weights[...], preferred_element_type=F32)
        edge = jnp.zeros((rows, ch), F32)
        before = jnp.concatenate([edge, taps[0:cells - rows, 0:ch]], axis=0)
        after = jnp.concatenate([taps[rows:, 2 * ch:], edge], axis=0)
        return taps[:, ch:2 * ch] + before + after

    def as_f32(column):
        return column.reshape(cells, ch).astype(F32)

    for copy in x_loads:
        copy.wait()
    for w in range(cols):
        widen(as_f32(xb[w + 1]), x3, w + 1)
        flip(x3, w + 1, xt)
    if scatter:
        pl.semaphore_wait(barrier, len(peers))
    else:
        pl.semaphore_wait(barrier, 2)
    start(x_swap, 0)
    start(x_swap, 1)

    for copy in w_loads + up_loads + [bias_load]:
        copy.wait()
    for a in range(3):
        for b in range(3):
            for c in range(3):
                row = wide * (2 - b) + ch * (2 - c)
                wt[wide * b + ch * c:wide * b + ch * (c + 1), ch * a:ch * (a + 1)] = wv[
                    row:row + ch, ch * (2 - a):ch * (3 - a)
                ].T

    def forward(w):
        hidden = conv(x3, wv, w) + bias_ref[...]
        sigma = jax.nn.sigmoid(hidden)
        sig[w] = sigma
        value = (as_f32(upb[w]) * (0.2 + 0.8 * sigma)).astype(BF16)
        ghp[w, 1:frames + 1] = value.reshape(frames, rows, ch)
        return value

    inner = list(range(1, cols - 1))
    for w in inner:
        widen(forward(w).astype(F32), h3, w + 1)
    for side in range(2):
        w = 0 if side == 0 else cols - 1
        halo = 0 if side == 0 else cols + 1
        finish_recv(x_swap, side)
        widen(as_f32(xb[halo]), x3, halo)
        value = forward(w)
        hs[side] = value.reshape(frames, rows, ch)
        start(h_swap, side)
    for side in range(2):
        widen(as_f32(hs[side]), h3, 1 if side == 0 else cols)
    flip(x3, 0, xt)
    flip(x3, cols + 1, xt)

    def backward(w):
        value = conv(h3, wt, w)
        squares = jnp.sum(value * value, axis=0, keepdims=True)
        return value.astype(BF16), squares

    squares = jnp.zeros((1, ch), F32)
    for w in inner:
        value, add = backward(w)
        squares = squares + add
        widen(value.astype(F32), g3, w + 1)
        flip(g3, w + 1, gt)
    for side in range(2):
        w = 0 if side == 0 else cols - 1
        halo = 0 if side == 0 else cols + 1
        finish_recv(h_swap, side)
        widen(as_f32(hr[side]), h3, halo)
        value, add = backward(w)
        squares = squares + add
        gs[side] = value.reshape(frames, rows, ch)
        start(g_swap, side)
    for side in range(2):
        w = 0 if side == 0 else cols - 1
        widen(as_f32(gs[side]), g3, w + 1)
        flip(g3, w + 1, gt)

    def curve(w):
        sigma = sig[w]
        value = (conv(g3, wv, w) * as_f32(upb[w]) * (0.8 * sigma * (1.0 - sigma))).astype(BF16)
        cvp[w, 1:frames + 1] = value.reshape(frames, rows, ch)
        return jnp.sum(value.astype(F32), axis=0, keepdims=True)

    if scatter:
        pf = scratch[28]
    units = [((0, 2), b) for b in range(3)] + [((1,), b) for b in range(3)]

    def places(g):
        at = wide * g
        while at < wide * (g + 1):
            owner = at // block
            end = min(wide * (g + 1), (owner + 1) * block)
            if scatter:
                place = (owner, slice(at - owner * block, end - owner * block))
            else:
                place = (slice(at, end),)
            yield place, at - wide * g, end - wide * g
            at = end

    def near(b):
        return [w for w in range(cols) if 1 <= w + b <= cols]

    def columns(pads, lo, hi, a):
        return pads[lo:hi, 2 - a:2 - a + deep].reshape((hi - lo) * lanes, ch)

    sums = pf if scatter else out_ref

    def terms_near(unit):
        taps, b = unit
        lo, hi = near(b)[0], near(b)[-1] + 1
        right = jnp.concatenate([columns(ghp, lo, hi, a) for a in taps], axis=1)
        value = jnp.dot(gt[:, (lo + b) * lanes:(hi + b) * lanes], right, preferred_element_type=F32)
        for n, a in enumerate(taps):
            for place, lo_row, hi_row in places(3 * a + b):
                sums[place] = value[lo_row:hi_row, n * ch:(n + 1) * ch]

    def terms_rest(unit):
        taps, b = unit
        far = [w for w in range(cols) if w not in near(b)]
        left = jnp.concatenate(
            [xt[:, b * lanes:(b + cols) * lanes]] + [gt[:, (w + b) * lanes:(w + b + 1) * lanes] for w in far],
            axis=1,
        )
        right = jnp.concatenate(
            [
                jnp.concatenate(
                    [columns(cvp, 0, cols, a)] + [columns(ghp, w, w + 1, a) for w in far], axis=0
                )
                for a in taps
            ],
            axis=1,
        )
        value = jnp.dot(left, right, preferred_element_type=F32)
        for n, a in enumerate(taps):
            for place, lo_row, hi_row in places(3 * a + b):
                sums[place] = sums[place] + value[lo_row:hi_row, n * ch:(n + 1) * ch]

    bias_sum = jnp.zeros((1, ch), F32)
    for w in inner:
        bias_sum = bias_sum + curve(w)
    for unit in units:
        terms_near(unit)
    for side in range(2):
        w = 0 if side == 0 else cols - 1
        halo = 0 if side == 0 else cols + 1
        finish_recv(g_swap, side)
        widen(as_f32(gr[side]), g3, halo)
        flip(g3, halo, gt)
        bias_sum = bias_sum + curve(w)
    st[...] = jnp.zeros_like(st)
    st[0:1, :] = bias_sum
    st[1:2, :] = squares

    if not scatter:
        for unit in units:
            terms_rest(unit)
        stat_ref[...] = st[...]
    else:
        (pf, pr, pb, rb, zb, rz, own, og, sr, s2, sb, sz, pair_send, pair_recv, sc_send, sc_recv,
         z_send, z_recv, ag_send, ag_recv, stat_send, stat_recv) = scratch[28:]
        half = tiles // 2
        core = lax.rem(t, 2)
        z = t // 2
        other = t + 1 - 2 * core

        def remote(src, dst, send_sem, recv_sem, device):
            return pltpu.make_async_remote_copy(
                src_ref=src, dst_ref=dst, send_sem=send_sem, recv_sem=recv_sem,
                device_id=device, device_id_type=MESH,
            )

        def clip_at(step):
            return lax.rem(k + step, clips)

        def z_at(step):
            return lax.rem(z + step, half)

        stat_pair = remote(st, sr, stat_send.at[0], stat_recv.at[0], (k, other))
        stat_clip = [
            remote(s2, sb.at[k], stat_send.at[dk], stat_recv.at[1 + k], (clip_at(dk), t))
            for dk in range(1, clips)
        ]
        stat_z = [
            remote(sb.at[k], sz.at[z], stat_send.at[clips + dz], stat_recv.at[1 + clips + z],
                   (k, 2 * z_at(dz) + core))
            for dz in range(1, half)
        ]

        def stats_a():
            stat_pair.wait_recv()
            s2[...] = st[...] + sr[...]
            for copy in stat_clip:
                copy.start()

        def stats_b():
            total = s2[...]
            for dk in range(1, clips):
                slot = clip_at(dk)
                remote(s2, sb.at[slot], stat_send.at[dk], stat_recv.at[1 + slot], (slot, t)).wait_recv()
                total = total + sb[slot]
            sb[k] = total
            for copy in stat_z:
                copy.start()

        def stats_c():
            total = sb[k]
            for dz in range(1, half):
                slot = z_at(dz)
                remote(
                    sb.at[k], sz.at[slot], stat_send.at[clips + dz], stat_recv.at[1 + clips + slot],
                    (k, 2 * slot + core),
                ).wait_recv()
                total = total + sz[slot]
            bias_ref_out[...] = factor * total[0:1, :]
            pen_ref[...] = 0.5 * factor * jnp.sum(total[1:2, :], axis=1, keepdims=True)

        stat_pair.start()
        pf[:, block:, :] = jnp.zeros((tiles, pf.shape[1] - block, ch), F32)
        pr[:, block:, :] = jnp.zeros((half, pf.shape[1] - block, ch), F32)

        def ready(j):
            lo, hi = 2 * j * block, (2 * j + 2) * block
            return set(range(lo // wide, (hi - 1) // wide + 1))

        pairs = [
            remote(pf.at[2 * j + 1 - core, 0:block], pr.at[j, 0:block], pair_send.at[j], pair_recv.at[j],
                   (k, other))
            for j in range(half)
        ]
        clip_sends = [
            [
                remote(pb.at[j, clip_at(dk)], rb.at[j, k], sc_send.at[j, dk], sc_recv.at[j, k],
                       (clip_at(dk), t))
                for dk in range(1, clips)
            ]
            for j in range(half)
        ]
        z_sends = [
            remote(zb.at[j], rz.at[z], z_send.at[j], z_recv.at[z], (k, 2 * j + core)) for j in range(half)
        ]

        def over_clips(j):
            pairs[j].wait_recv()
            summed = pf[2 * j + core] + pr[j]
            pf[2 * j + core] = summed
            pb[j] = summed.astype(BF16).reshape(clips, piece, ch)
            for copy in clip_sends[j]:
                copy.start()

        def over_z(j):
            total = pf[2 * j + core, pl.ds(pl.multiple_of(k * piece, 16), piece), :]
            for dk in range(1, clips):
                slot = clip_at(dk)
                remote(pb.at[j, slot], rb.at[j, slot], sc_send.at[j, dk], sc_recv.at[j, slot],
                       (slot, t)).wait_recv()
                total = total + rb[j, slot].astype(F32)

            @pl.when(z == j)
            def _():
                own[...] = total

            @pl.when(z != j)
            def _():
                zb[j] = total.astype(BF16)
                z_sends[j].start()

        done, begun, paired = set(), [], []
        for n, unit in enumerate(units):
            terms_rest(unit)
            done |= {3 * a + unit[1] for a in unit[0]}
            fresh = [j for j in range(half) if j not in begun and ready(j) <= done]
            for j in fresh:
                pairs[j].start()
            if n == 1:
                stats_a()
            for j in paired:
                over_clips(j)
            begun += fresh
            paired = fresh
        for j in paired:
            over_clips(j)
        stats_b()
        for j in begun:
            over_z(j)

        total = own[...]
        for dz in range(1, half):
            slot = z_at(dz)
            remote(zb.at[0], rz.at[slot], z_send.at[0], z_recv.at[slot], (k, 2 * slot + core)).wait_recv()
            total = total + rz[slot].astype(F32)
        og[k] = factor * total
        gathers = [
            remote(og.at[k], og.at[k], ag_send.at[dk], ag_recv.at[k], (clip_at(dk), t))
            for dk in range(1, clips)
        ]
        for copy in gathers:
            copy.start()
        stats_c()
        for dk in range(1, clips):
            slot = clip_at(dk)
            remote(og.at[slot], og.at[slot], ag_send.at[dk], ag_recv.at[slot], (slot, t)).wait_recv()
        out_ref[...] = og[...].reshape(clips * piece, ch)[0:block]
        for copy in gathers + stat_clip + stat_z + [stat_pair] + pairs:
            copy.wait_send()
        for j in range(half):
            for copy in clip_sends[j]:
                copy.wait_send()
            pl.when(z != j)(z_sends[j].wait_send)
    finish_send(x_swap)
    finish_send(h_swap)
    finish_send(g_swap)


def shards(clip_features, upstream, weight, conv_bias):
    count, frames, cols, rows, ch = clip_features.shape
    clips = lax.axis_size("clip")
    tiles = lax.axis_size("tile")
    factor = r1_weight / (count * clips * frames * rows * cols * tiles)
    weight_rows = weight.shape[0] * ch
    block = weight_rows // tiles
    scatter = block % 16 == 0 and tiles % 2 == 0
    piece = -(-block // (16 * clips)) * 16
    wide = 3 * ch
    lane_frames = 128 // rows
    deep = -(-frames // lane_frames) * lane_frames
    geo = (clips, tiles, frames, cols, rows, ch, block, piece, scatter, factor)
    dma = pltpu.SemaphoreType.DMA
    field = pltpu.VMEM((cols + 2, deep, rows, wide), BF16)
    flipped = pltpu.VMEM((wide, (cols + 2) * deep * rows), BF16)
    thin = pltpu.VMEM((cols, deep + 2, rows, ch), BF16)
    edge = pltpu.VMEM((2, frames, rows, ch), BF16)
    scratch = [
        pltpu.VMEM((1, ch), F32), dma,
        pltpu.VMEM((cols + 2, frames, rows, ch), BF16),
        pltpu.VMEM((cols, frames, rows, ch), BF16),
        pltpu.VMEM((3 * wide, wide), BF16),
        pltpu.VMEM((3 * wide, wide), BF16),
        field, field, field, flipped, flipped, thin, thin,
        pltpu.VMEM((cols, frames * rows, ch), F32),
        edge, edge, edge, edge,
        pltpu.VMEM((8, ch), F32),
        dma((cols,)), dma((cols,)), dma((9,)),
        dma((2,)), dma((2,)), dma((2,)), dma((2,)), dma((2,)), dma((2,)),
    ]
    half = tiles // 2
    out_rows = weight_rows
    if scatter:
        out_rows = block
        scratch += [
            pltpu.VMEM((tiles, clips * piece, ch), F32),
            pltpu.VMEM((half, clips * piece, ch), F32),
            pltpu.VMEM((half, clips, piece, ch), BF16),
            pltpu.VMEM((half, clips, piece, ch), BF16),
            pltpu.VMEM((half, piece, ch), BF16),
            pltpu.VMEM((half, piece, ch), BF16),
            pltpu.VMEM((piece, ch), F32),
            pltpu.VMEM((clips, piece, ch), F32),
            pltpu.VMEM((8, ch), F32),
            pltpu.VMEM((8, ch), F32),
            pltpu.VMEM((clips, 8, ch), F32),
            pltpu.VMEM((half, 8, ch), F32),
            dma((half,)), dma((half,)), dma((half, clips)), dma((half, clips)),
            dma((half,)), dma((half,)), dma((clips,)), dma((clips,)),
            dma((clips + half,)), dma((1 + clips + half,)),
        ]
    hbm = pl.BlockSpec(memory_space=pltpu.HBM)
    vmem = pl.BlockSpec(memory_space=pltpu.VMEM)
    outs = (jax.ShapeDtypeStruct((out_rows, ch), F32), jax.ShapeDtypeStruct((8, ch), F32))
    if scatter:
        outs = (pltpu.VMEM((out_rows, ch), F32), pltpu.VMEM((1, ch), F32), jax.ShapeDtypeStruct((1, 1), F32))
    results = pl.pallas_call(
        functools.partial(kernel, geo),
        out_shape=outs,
        in_specs=[hbm, hbm, hbm, hbm],
        out_specs=(vmem,) * len(outs),
        scratch_shapes=scratch,
        compiler_params=pltpu.CompilerParams(
            collective_id=0, has_side_effects=True, vmem_limit_bytes=60 * 1024 * 1024
        ),
        name="r1_section",
    )(
        clip_features.reshape(frames, cols, rows, ch),
        upstream.reshape(frames, cols, rows, ch),
        weight.reshape(9, wide, ch),
        conv_bias.reshape(1, ch),
    )
    if scatter:
        return results[0], results[1].reshape(ch), results[2].reshape(())
    grads, stats = results
    grads = factor * lax.psum(lax.psum_scatter(grads, "tile", scatter_dimension=0, tiled=True), "clip")
    stats = lax.psum(stats, ("clip", "tile"))
    return grads, factor * stats[0], 0.5 * factor * jnp.sum(stats[1])


def solution(mesh):
    in_specs = (P("clip", None, "tile", None, None), P("clip", None, "tile", None, None), P(), P())
    out_specs = (P("tile", None), P(), P())
    return jax.shard_map(shards, mesh=mesh, in_specs=in_specs, out_specs=out_specs, check_vma=False)
```

```python
import functools

import jax
import jax.numpy as jnp
from jax import lax
from jax.experimental import pallas as pl
from jax.experimental.pallas import tpu as pltpu
from jax.sharding import PartitionSpec as P

r1_weight = 10.0
MESH = pl.DeviceIdType.MESH
BF16 = jnp.bfloat16
F32 = jnp.float32
SHARE = 75


def kernel(geo, x_hbm, up_hbm, w_hbm, bias_hbm, out_ref, *rest):
    (clips, tiles, frames, cols, rows, ch, block, piece, scatter, factor) = geo
    if scatter:
        bias_out, pen_ref, *scratch = rest
    else:
        stat_ref, *scratch = rest
    (bias_ref, xb, upb, wv, wt, x3, h3, g3, xt, gt, ghp, cvp, sig, hr, gs, gr, st,
     bias_sem, load_sem, up_sem, w_sem, near_send, near_recv, far_send, far_recv) = scratch[:25]
    k = lax.axis_index("clip")
    t = lax.axis_index("tile")
    core = lax.rem(t, 2)
    other = t + 1 - 2 * core
    outer = t - 1 + 2 * core
    has_outer = jnp.logical_and(outer >= 0, outer < tiles)
    outer_at = (k, jnp.clip(outer, 0, tiles - 1))
    cells = frames * rows
    wide = 3 * ch
    deep = x3.shape[1]
    lanes = deep * rows

    def column_at(q):
        return cols - 1 - q + core * (2 * q - cols + 1)

    def tap_at(b):
        return 2 - b + core * (2 * b - 2)

    peers = [(0, dt) for dt in range(1, tiles)] + [(dk, 0) for dk in range(1, clips)]
    barrier = pltpu.get_barrier_semaphore()
    if scatter:
        for dk, dt in peers:
            pl.semaphore_signal(
                barrier, inc=1,
                device_id=(lax.rem(k + dk, clips), lax.rem(t + dt, tiles)), device_id_type=MESH,
            )
    else:
        for step in (1, tiles - 1):
            pl.semaphore_signal(
                barrier, inc=1, device_id=(k, lax.rem(t + step, tiles)), device_id_type=MESH
            )

    x_loads = [
        pltpu.make_async_copy(x_hbm.at[:, column_at(q)], xb.at[q + 1], load_sem.at[q]) for q in range(cols)
    ]
    for copy in x_loads:
        copy.start()
    w_loads = [
        pltpu.make_async_copy(
            w_hbm.at[3 * a + tap_at(b)], wv.at[wide * b:wide * (b + 1), a * ch:(a + 1) * ch],
            w_sem.at[3 * a + b],
        )
        for a in range(3)
        for b in range(3)
    ]
    for copy in w_loads:
        copy.start()
    up_loads = [
        pltpu.make_async_copy(up_hbm.at[:, column_at(q)], upb.at[q], up_sem.at[q]) for q in range(cols)
    ]
    for copy in up_loads:
        copy.start()
    bias_load = pltpu.make_async_copy(bias_hbm, bias_ref, bias_sem)
    bias_load.start()

    def remote(src, dst, send_sem, recv_sem, device):
        return pltpu.make_async_remote_copy(
            src_ref=src, dst_ref=dst, send_sem=send_sem, recv_sem=recv_sem,
            device_id=device, device_id_type=MESH,
        )

    def to_other(n, src, dst):
        return remote(src, dst, near_send.at[n], near_recv.at[n], (k, other))

    def to_outer(n, src, dst):
        return remote(src, dst, far_send.at[n], far_recv.at[n], outer_at)

    x_near = to_other(0, x_hbm.at[:, column_at(0)], xb.at[0])
    h_near = to_other(1, ghp.at[0, 1:frames + 1], hr)
    g_near = to_other(2, gs, gr)
    x_far = [to_outer(i, x_hbm.at[:, column_at(cols - 1 - i)], xb.at[cols + 1 + i]) for i in range(3)]
    up_far = [to_outer(3 + i, up_hbm.at[:, column_at(cols - 1 - i)], upb.at[cols + i]) for i in range(2)]

    def when_outer(*steps):
        @pl.when(has_outer)
        def _():
            for step in steps:
                step()

    zero_wide = jnp.zeros((rows, wide), BF16)
    for field in (x3, g3):
        for w in range(cols + 2):
            for f in range(frames, deep):
                field[w, f] = zero_wide
    zero_thin = jnp.zeros((rows, ch), BF16)
    for field in (ghp, cvp):
        for w in range(cols):
            for f in [0] + list(range(frames + 1, field.shape[1])):
                field[w, f] = zero_thin
    zero_col = jnp.zeros((frames, rows, ch), BF16)

    @pl.when(jnp.logical_not(has_outer))
    def _():
        for i in range(3):
            xb[cols + 1 + i] = zero_col
        for i in range(2):
            upb[cols + i] = zero_col

    if scatter:
        pl.semaphore_wait(barrier, len(peers))
    else:
        pl.semaphore_wait(barrier, 2)
    x_near.start()
    when_outer(x_far[0].start, x_far[1].start, up_far[0].start, x_far[2].start, up_far[1].start)

    row_at = lax.rem(lax.broadcasted_iota(jnp.int32, (cells, ch), 0), rows)
    first_row = row_at == 0
    last_row = row_at == rows - 1

    def widen(value, field, w):
        before = jnp.where(first_row, 0.0, pltpu.roll(value, 1, 0)).astype(BF16)
        after = jnp.where(last_row, 0.0, pltpu.roll(value, cells - 1, 0)).astype(BF16)
        shape = (frames, rows, ch)
        field[w, 0:frames, :, 0:ch] = before.reshape(shape)
        field[w, 0:frames, :, ch:2 * ch] = value.astype(BF16).reshape(shape)
        field[w, 0:frames, :, 2 * ch:] = after.reshape(shape)

    def flip(field, w, target):
        target[:, w * lanes:(w + 1) * lanes] = field[w].reshape(lanes, wide).T

    def conv(field, weights, q):
        left = jnp.concatenate(
            [field[q + b, 0:frames].reshape(cells, wide) for b in range(3)], axis=1
        )
        taps = jnp.dot(left, weights[...], preferred_element_type=F32)
        edge = jnp.zeros((rows, ch), F32)
        before = jnp.concatenate([edge, taps[0:cells - rows, 0:ch]], axis=0)
        after = jnp.concatenate([taps[rows:, 2 * ch:], edge], axis=0)
        return taps[:, ch:2 * ch] + before + after

    def as_f32(column):
        return column.reshape(cells, ch).astype(F32)

    def forward(q):
        hidden = conv(x3, wv, q) + bias_ref[...]
        sigma = jax.nn.sigmoid(hidden)
        value = (as_f32(upb[q]) * (0.2 + 0.8 * sigma)).astype(BF16)
        if q < cols:
            sig[q] = sigma
            ghp[q, 1:frames + 1] = value.reshape(frames, rows, ch)
        widen(value.astype(F32), h3, q + 1)

    def backward(q):
        value = conv(h3, wt, q)
        if q == cols:
            value = jnp.where(has_outer, value, 0.0)
        if q == 0:
            gs[...] = value.astype(BF16).reshape(frames, rows, ch)
        widen(value.astype(BF16).astype(F32), g3, q + 1)
        return jnp.sum(value * value, axis=0, keepdims=True)

    def curve(q):
        sigma = sig[q]
        value = (conv(g3, wv, q) * as_f32(upb[q]) * (0.8 * sigma * (1.0 - sigma))).astype(BF16)
        cvp[q, 1:frames + 1] = value.reshape(frames, rows, ch)
        return jnp.sum(value.astype(F32), axis=0, keepdims=True)

    for copy in x_loads:
        copy.wait()
    for q in range(cols):
        widen(as_f32(xb[q + 1]), x3, q + 1)
    for copy in w_loads + up_loads + [bias_load]:
        copy.wait()
    inner = list(range(1, cols - 1))
    for q in inner:
        forward(q)
    for a in range(3):
        for b in range(3):
            for c in range(3):
                row = wide * (2 - b) + ch * (2 - c)
                wt[wide * b + ch * c:wide * b + ch * (c + 1), ch * a:ch * (a + 1)] = wv[
                    row:row + ch, ch * (2 - a):ch * (3 - a)
                ].T
    for q in range(cols):
        flip(x3, q + 1, xt)
    x_near.wait_recv()
    widen(as_f32(xb[0]), x3, 0)
    forward(0)
    h_near.start()
    flip(x3, 0, xt)

    when_outer(x_far[0].wait_recv)
    widen(as_f32(xb[cols + 1]), x3, cols + 1)
    forward(cols - 1)
    squares = jnp.zeros((1, ch), F32)
    for q in inner:
        squares = squares + backward(q)
    flip(x3, cols + 1, xt)
    h_near.wait_recv()
    widen(as_f32(hr[...]), h3, 0)
    squares = squares + backward(0)
    g_near.start()
    when_outer(x_far[1].wait_recv, up_far[0].wait_recv)
    widen(as_f32(xb[cols + 2]), x3, cols + 2)
    forward(cols)
    squares = squares + backward(cols - 1)
    for q in range(cols):
        flip(g3, q + 1, gt)

    units = [((0, 2), b) for b in range(3)] + [((1,), b) for b in range(3)]

    def near(b):
        return [w for w in range(cols) if 1 <= w + b <= cols]

    def columns(pads, lo, hi, a):
        return pads[lo:hi, 2 - a:2 - a + deep].reshape((hi - lo) * lanes, ch)

    sums = scratch[25] if scatter else out_ref

    def place(a, b):
        return pl.ds(pl.multiple_of(wide * (3 * a + tap_at(b)), ch), wide)

    def terms_near(unit):
        taps, b = unit
        lo, hi = near(b)[0], near(b)[-1] + 1
        right = jnp.concatenate([columns(ghp, lo, hi, a) for a in taps], axis=1)
        value = jnp.dot(gt[:, (lo + b) * lanes:(hi + b) * lanes], right, preferred_element_type=F32)
        for n, a in enumerate(taps):
            sums[place(a, b), :] = value[:, n * ch:(n + 1) * ch]

    def terms_rest(unit):
        taps, b = unit
        far = [w for w in range(cols) if w not in near(b)]
        left = jnp.concatenate(
            [xt[:, b * lanes:(b + cols) * lanes]] + [gt[:, (w + b) * lanes:(w + b + 1) * lanes] for w in far],
            axis=1,
        )
        right = jnp.concatenate(
            [
                jnp.concatenate(
                    [columns(cvp, 0, cols, a)] + [columns(ghp, w, w + 1, a) for w in far], axis=0
                )
                for a in taps
            ],
            axis=1,
        )
        value = jnp.dot(left, right, preferred_element_type=F32)
        for n, a in enumerate(taps):
            sums[place(a, b), :] = sums[place(a, b), :] + value[:, n * ch:(n + 1) * ch]

    for unit in units:
        terms_near(unit)
    g_near.wait_recv()
    when_outer(x_far[2].wait_recv, up_far[1].wait_recv)
    widen(as_f32(gr[...]), g3, 0)
    widen(as_f32(xb[cols + 3]), x3, cols + 3)
    forward(cols + 1)
    bias_sum = jnp.zeros((1, ch), F32)
    for q in range(cols - 1):
        bias_sum = bias_sum + curve(q)
    backward(cols)
    flip(g3, 0, gt)
    flip(g3, cols + 1, gt)
    bias_sum = bias_sum + curve(cols - 1)
    st[...] = jnp.zeros_like(st)
    st[0:1, :] = bias_sum
    st[1:2, :] = squares

    if not scatter:
        for unit in units:
            terms_rest(unit)
        stat_ref[...] = st[...]
    else:
        (pf, pr, pb, rb, zb, rz, own, og, qb, rq, qown, qc, sr, s2, sb, sz, pair_send, pair_recv, sc_send,
         sc_recv, z_send, z_recv, ag_send, ag_recv, q_send, q_recv, qc_send, qc_recv, stat_send,
         stat_recv) = scratch[25:]
        half = tiles // 2
        z = t // 2
        thick = clips * piece

        def clip_at(step):
            return lax.rem(k + step, clips)

        def z_at(step):
            return lax.rem(z + step, half)

        def block_at(tile, start, size):
            return pl.ds(pl.multiple_of(tile * block + start, 16), size)

        stat_pair = remote(st, sr, stat_send.at[0], stat_recv.at[0], (k, other))
        stat_clip = [
            remote(s2, sb.at[k], stat_send.at[dk], stat_recv.at[1 + k], (clip_at(dk), t))
            for dk in range(1, clips)
        ]
        stat_z = [
            remote(sb.at[k], sz.at[z], stat_send.at[clips + dz], stat_recv.at[1 + clips + z],
                   (k, 2 * z_at(dz) + core))
            for dz in range(1, half)
        ]

        def stats_a():
            stat_pair.wait_recv()
            s2[...] = st[...] + sr[...]
            for copy in stat_clip:
                copy.start()

        def stats_b():
            total = s2[...]
            for dk in range(1, clips):
                slot = clip_at(dk)
                remote(s2, sb.at[slot], stat_send.at[dk], stat_recv.at[1 + slot], (slot, t)).wait_recv()
                total = total + sb[slot]
            sb[k] = total
            for copy in stat_z:
                copy.start()

        def stats_c():
            total = sb[k]
            for dz in range(1, half):
                slot = z_at(dz)
                remote(
                    sb.at[k], sz.at[slot], stat_send.at[clips + dz], stat_recv.at[1 + clips + slot],
                    (k, 2 * slot + core),
                ).wait_recv()
                total = total + sz[slot]
            bias_out[...] = factor * total[0:1, :]
            pen_ref[...] = 0.5 * factor * jnp.sum(total[1:2, :], axis=1, keepdims=True)

        stat_pair.start()

        def ready(j):
            lo, hi = 2 * j * block, (2 * j + 2) * block
            return set(range(lo // wide, (hi - 1) // wide + 1))

        pairs = [
            remote(pf.at[block_at(2 * j + 1 - core, 0, block)], pr.at[j], pair_send.at[j], pair_recv.at[j],
                   (k, other))
            for j in range(half)
        ]
        clip_sends = [
            [
                remote(pb.at[j, clip_at(dk)], rb.at[j, k], sc_send.at[j, dk], sc_recv.at[j, k],
                       (clip_at(dk), t))
                for dk in range(1, clips)
            ]
            for j in range(half)
        ]
        z_sends = [
            remote(zb.at[j], rz.at[z], z_send.at[j], z_recv.at[z], (k, 2 * j + core)) for j in range(half)
        ]
        q_sends = [
            remote(qb.at[j], rq.at[z], q_send.at[j], q_recv.at[z], (k, 2 * j + core)) for j in range(half)
        ]

        def after_pair(j):
            pairs[j].wait_recv()
            first = pf[block_at(2 * j + core, 0, thick), :] + pr[j, 0:thick]
            pf[block_at(2 * j + core, 0, thick), :] = first
            pb[j] = first.astype(BF16).reshape(clips, piece, ch)
            for copy in clip_sends[j]:
                copy.start()
            second = pf[block_at(2 * j + core, thick, block - thick), :] + pr[j, thick:block]

            @pl.when(z == j)
            def _():
                qown[...] = second

            @pl.when(z != j)
            def _():
                qb[j] = second.astype(BF16)
                q_sends[j].start()

        def over_z(j):
            total = pf[block_at(2 * j + core, k * piece, piece), :]
            for dk in range(1, clips):
                slot = clip_at(dk)
                remote(pb.at[j, slot], rb.at[j, slot], sc_send.at[j, dk], sc_recv.at[j, slot],
                       (slot, t)).wait_recv()
                total = total + rb[j, slot].astype(F32)

            @pl.when(z == j)
            def _():
                own[...] = total

            @pl.when(z != j)
            def _():
                zb[j] = total.astype(BF16)
                z_sends[j].start()

        done, begun, paired = (set(), set()), [], []
        for n, part in enumerate((units[:3], units[3:])):
            for unit in part:
                terms_rest(unit)
                for a in unit[0]:
                    done[0].add(3 * a + unit[1])
                    done[1].add(3 * a + 2 - unit[1])
            fresh = [j for j in range(half) if j not in begun and ready(j) <= done[0] & done[1]]
            for j in fresh:
                pairs[j].start()
            if n == 0:
                stats_a()
            for j in paired:
                after_pair(j)
            begun += fresh
            paired = fresh
        for j in paired:
            after_pair(j)
        stats_b()
        for j in begun:
            over_z(j)

        total = qown[...]
        for dz in range(1, half):
            slot = z_at(dz)
            remote(qb.at[0], rq.at[slot], q_send.at[0], q_recv.at[slot], (k, 2 * slot + core)).wait_recv()
            total = total + rq[slot].astype(F32)
        qc[k] = total.astype(BF16)
        spreads = [
            remote(qc.at[k], qc.at[k], qc_send.at[dk], qc_recv.at[k], (clip_at(dk), t))
            for dk in range(1, clips)
        ]
        for copy in spreads:
            copy.start()

        total = own[...]
        for dz in range(1, half):
            slot = z_at(dz)
            remote(zb.at[0], rz.at[slot], z_send.at[0], z_recv.at[slot], (k, 2 * slot + core)).wait_recv()
            total = total + rz[slot].astype(F32)
        og[k] = factor * total
        gathers = [
            remote(og.at[k], og.at[k], ag_send.at[dk], ag_recv.at[k], (clip_at(dk), t))
            for dk in range(1, clips)
        ]
        for copy in gathers:
            copy.start()
        stats_c()
        for dk in range(1, clips):
            slot = clip_at(dk)
            remote(qc.at[slot], qc.at[slot], qc_send.at[dk], qc_recv.at[slot], (slot, t)).wait_recv()
        total = qc[0].astype(F32)
        for slot in range(1, clips):
            total = total + qc[slot].astype(F32)
        out_ref[thick:block, :] = factor * total
        for dk in range(1, clips):
            slot = clip_at(dk)
            remote(og.at[slot], og.at[slot], ag_send.at[dk], ag_recv.at[slot], (slot, t)).wait_recv()
        out_ref[0:thick, :] = og[...].reshape(thick, ch)
        for copy in gathers + spreads + stat_clip + stat_z + [stat_pair] + pairs:
            copy.wait_send()
        for j in range(half):
            for copy in clip_sends[j]:
                copy.wait_send()

            @pl.when(z != j)
            def _():
                z_sends[j].wait_send()
                q_sends[j].wait_send()
    for copy in (x_near, h_near, g_near):
        copy.wait_send()
    when_outer(*[copy.wait_send for copy in x_far + up_far])


def shards(clip_features, upstream, weight, conv_bias):
    count, frames, cols, rows, ch = clip_features.shape
    clips = lax.axis_size("clip")
    tiles = lax.axis_size("tile")
    factor = r1_weight / (count * clips * frames * rows * cols * tiles)
    weight_rows = weight.shape[0] * ch
    block = weight_rows // tiles
    scatter = block % 16 == 0
    piece = max(1, block * SHARE // (1600 * clips)) * 16
    wide = 3 * ch
    lane_frames = 128 // rows
    deep = -(-frames // lane_frames) * lane_frames
    geo = (clips, tiles, frames, cols, rows, ch, block, piece, scatter, factor)
    dma = pltpu.SemaphoreType.DMA

    def field(width, depth):
        return pltpu.VMEM((width, depth, rows, wide), BF16)

    flipped = pltpu.VMEM((wide, (cols + 2) * deep * rows), BF16)
    thin = pltpu.VMEM((cols, deep + 2, rows, ch), BF16)
    edge = pltpu.VMEM((frames, rows, ch), BF16)
    scratch = [
        pltpu.VMEM((1, ch), F32),
        pltpu.VMEM((cols + 4, frames, rows, ch), BF16),
        pltpu.VMEM((cols + 2, frames, rows, ch), BF16),
        pltpu.VMEM((3 * wide, wide), BF16),
        pltpu.VMEM((3 * wide, wide), BF16),
        field(cols + 4, deep), field(cols + 3, frames), field(cols + 2, deep), flipped, flipped, thin, thin,
        pltpu.VMEM((cols, frames * rows, ch), F32),
        edge, edge, edge,
        pltpu.VMEM((8, ch), F32),
        dma, dma((cols,)), dma((cols,)), dma((9,)), dma((3,)), dma((3,)), dma((5,)), dma((5,)),
    ]
    half = tiles // 2
    out_rows = weight_rows
    if scatter:
        out_rows = block
        others = block - clips * piece
        scratch += [
            pltpu.VMEM((weight_rows, ch), F32),
            pltpu.VMEM((half, block, ch), F32),
            pltpu.VMEM((half, clips, piece, ch), BF16),
            pltpu.VMEM((half, clips, piece, ch), BF16),
            pltpu.VMEM((half, piece, ch), BF16),
            pltpu.VMEM((half, piece, ch), BF16),
            pltpu.VMEM((piece, ch), F32),
            pltpu.VMEM((clips, piece, ch), F32),
            pltpu.VMEM((half, others, ch), BF16),
            pltpu.VMEM((half, others, ch), BF16),
            pltpu.VMEM((others, ch), F32),
            pltpu.VMEM((clips, others, ch), BF16),
            pltpu.VMEM((8, ch), F32),
            pltpu.VMEM((8, ch), F32),
            pltpu.VMEM((clips, 8, ch), F32),
            pltpu.VMEM((half, 8, ch), F32),
            dma((half,)), dma((half,)), dma((half, clips)), dma((half, clips)),
            dma((half,)), dma((half,)), dma((clips,)), dma((clips,)),
            dma((half,)), dma((half,)), dma((clips,)), dma((clips,)),
            dma((clips + half,)), dma((1 + clips + half,)),
        ]
    hbm = pl.BlockSpec(memory_space=pltpu.HBM)
    vmem = pl.BlockSpec(memory_space=pltpu.VMEM)
    outs = (jax.ShapeDtypeStruct((out_rows, ch), F32), jax.ShapeDtypeStruct((8, ch), F32))
    if scatter:
        outs = (pltpu.VMEM((out_rows, ch), F32), pltpu.VMEM((1, ch), F32), jax.ShapeDtypeStruct((1, 1), F32))
    results = pl.pallas_call(
        functools.partial(kernel, geo),
        out_shape=outs,
        in_specs=[hbm, hbm, hbm, hbm],
        out_specs=(vmem,) * len(outs),
        scratch_shapes=scratch,
        compiler_params=pltpu.CompilerParams(
            collective_id=0, has_side_effects=True, vmem_limit_bytes=60 * 1024 * 1024
        ),
        name="r1_section",
    )(
        clip_features.reshape(frames, cols, rows, ch),
        upstream.reshape(frames, cols, rows, ch),
        weight.reshape(9, wide, ch),
        conv_bias.reshape(1, ch),
    )
    if scatter:
        return results[0], results[1].reshape(ch), results[2].reshape(())
    grads, stats = results
    grads = factor * lax.psum(lax.psum_scatter(grads, "tile", scatter_dimension=0, tiled=True), "clip")
    stats = lax.psum(stats, ("clip", "tile"))
    return grads, factor * stats[0], 0.5 * factor * jnp.sum(stats[1])


def solution(mesh):
    in_specs = (P("clip", None, "tile", None, None), P("clip", None, "tile", None, None), P(), P())
    out_specs = (P("tile", None), P(), P())
    return jax.shard_map(shards, mesh=mesh, in_specs=in_specs, out_specs=out_specs, check_vma=False)
```

```python
import functools

import jax
import jax.numpy as jnp
from jax import lax
from jax.experimental import pallas as pl
from jax.experimental.pallas import tpu as pltpu
from jax.sharding import PartitionSpec as P

r1_weight = 10.0
MESH = pl.DeviceIdType.MESH
BF16 = jnp.bfloat16
F32 = jnp.float32
SHARE = 75


def kernel(geo, x_hbm, up_hbm, w_hbm, bias_hbm, out_ref, *rest):
    (clips, tiles, frames, cols, rows, ch, block, piece, scatter, factor) = geo
    if scatter:
        bias_out, pen_ref, *scratch = rest
    else:
        stat_ref, *scratch = rest
    (bias_ref, xb, upb, wv, ww, wt, wu, x3, h3, g3, xt, gt, xe, ge, ghp, cvp, sig, hr, gs, gr, st,
     bias_sem, load_sem, up_sem, w_sem, near_send, near_recv, far_send, far_recv) = scratch[:29]
    k = lax.axis_index("clip")
    t = lax.axis_index("tile")
    core = lax.rem(t, 2)
    other = t + 1 - 2 * core
    outer = t - 1 + 2 * core
    has_outer = jnp.logical_and(outer >= 0, outer < tiles)
    outer_at = (k, jnp.clip(outer, 0, tiles - 1))
    cells = frames * rows
    wide = 3 * ch
    last = 9 * ch - ch
    main = xt.shape[1] // ((cols + 2) * rows)
    lanes = main * rows

    def column_at(q):
        return cols - 1 - q + core * (2 * q - cols + 1)

    def tap_at(b):
        return 2 - b + core * (2 * b - 2)

    peers = [(0, dt) for dt in (1, tiles - 1)] + [(dk, 0) for dk in range(1, clips)]
    peers += [(0, dt) for dt in range(2, tiles - 1)]
    barrier = pltpu.get_barrier_semaphore()
    if scatter:
        for dk, dt in peers:
            pl.semaphore_signal(
                barrier, inc=1,
                device_id=(lax.rem(k + dk, clips), lax.rem(t + dt, tiles)), device_id_type=MESH,
            )
    else:
        for step in (1, tiles - 1):
            pl.semaphore_signal(
                barrier, inc=1, device_id=(k, lax.rem(t + step, tiles)), device_id_type=MESH
            )

    x_loads = [
        pltpu.make_async_copy(x_hbm.at[:, column_at(q)], xb.at[q + 1], load_sem.at[q]) for q in range(cols)
    ]
    for copy in x_loads:
        copy.start()
    w_loads = [
        pltpu.make_async_copy(
            w_hbm.at[3 * a + tap_at(b)], wv.at[wide * b:wide * (b + 1), a * ch:(a + 1) * ch],
            w_sem.at[3 * a + b],
        )
        for a in range(2)
        for b in range(3)
    ]
    w_loads += [
        pltpu.make_async_copy(w_hbm.at[6 + tap_at(b)], ww.at[wide * b:wide * (b + 1)], w_sem.at[6 + b])
        for b in range(2)
    ]
    w_loads += [
        pltpu.make_async_copy(w_hbm.at[6 + tap_at(2), 0:2 * ch], ww.at[2 * wide:last], w_sem.at[8]),
        pltpu.make_async_copy(
            w_hbm.at[6 + tap_at(2), 2 * ch:wide], wv.at[3 * wide:3 * wide + ch, ch:2 * ch], w_sem.at[9]
        ),
    ]
    for copy in w_loads:
        copy.start()
    up_loads = [
        pltpu.make_async_copy(up_hbm.at[:, column_at(q)], upb.at[q], up_sem.at[q]) for q in range(cols)
    ]
    for copy in up_loads:
        copy.start()
    bias_load = pltpu.make_async_copy(bias_hbm, bias_ref, bias_sem)
    bias_load.start()

    def remote(src, dst, send_sem, recv_sem, device):
        return pltpu.make_async_remote_copy(
            src_ref=src, dst_ref=dst, send_sem=send_sem, recv_sem=recv_sem,
            device_id=device, device_id_type=MESH,
        )

    def to_other(n, src, dst):
        return remote(src, dst, near_send.at[n], near_recv.at[n], (k, other))

    def to_outer(n, src, dst):
        return remote(src, dst, far_send.at[n], far_recv.at[n], outer_at)

    x_near = to_other(0, xb.at[1], xb.at[0])
    h_near = to_other(1, ghp.at[0, 1:frames + 1], hr)
    g_near = to_other(2, gs, gr)
    x_far = [to_outer(i, xb.at[cols - i], xb.at[cols + 1 + i]) for i in range(3)]
    up_far = [to_outer(3 + i, up_hbm.at[:, column_at(cols - 1 - i)], upb.at[cols + i]) for i in range(2)]

    def when_outer(*steps):
        @pl.when(has_outer)
        def _():
            for step in steps:
                step()

    if scatter:
        pl.semaphore_wait(barrier, len(peers))
    else:
        pl.semaphore_wait(barrier, 2)
    for copy in x_loads:
        copy.wait()
    x_near.start()
    when_outer(x_far[0].start, x_far[1].start, up_far[0].start, x_far[2].start, up_far[1].start)

    zero_wide = jnp.zeros((rows, wide), BF16)
    for field in (x3, h3, g3):
        for w in range(field.shape[0]):
            field[w, frames] = zero_wide
    zero_thin = jnp.zeros((rows, ch), BF16)
    for field in (ghp, cvp):
        for w in range(cols):
            for f in (0, frames + 1):
                field[w, f] = zero_thin
    for field in (wv, wt):
        field[3 * wide:, 0:ch] = jnp.zeros((ch, ch), BF16)
    zero_col = jnp.zeros((frames, rows, ch), BF16)

    @pl.when(jnp.logical_not(has_outer))
    def _():
        for i in range(3):
            xb[cols + 1 + i] = zero_col
        for i in range(2):
            upb[cols + i] = zero_col

    row_at = lax.rem(lax.broadcasted_iota(jnp.int32, (cells, ch), 0), rows)
    first_row = row_at == 0
    last_row = row_at == rows - 1

    def widen(value, field, w):
        before = jnp.where(first_row, 0.0, pltpu.roll(value, 1, 0)).astype(BF16)
        after = jnp.where(last_row, 0.0, pltpu.roll(value, cells - 1, 0)).astype(BF16)
        shape = (frames, rows, ch)
        field[w, 0:frames, :, 0:ch] = before.reshape(shape)
        field[w, 0:frames, :, ch:2 * ch] = value.astype(BF16).reshape(shape)
        field[w, 0:frames, :, 2 * ch:] = after.reshape(shape)

    def flip(field, w, target):
        target[:, w * lanes:(w + 1) * lanes] = field[w, 0:main].reshape(lanes, wide).T

    spare = frames - main
    ends = cols * spare * rows

    def flip_ends(field, b, target):
        parts = [field[w + b, main:frames].reshape(spare * rows, wide) for w in range(cols)]
        parts.append(jnp.zeros((target.shape[2] - ends, wide), BF16))
        target[b] = jnp.concatenate(parts, axis=0).T

    def conv(field, pair, single, q):
        left = jnp.concatenate(
            [field[q + b, 0:frames].reshape(cells, wide) for b in range(3)]
            + [field[q + 2, 1:frames + 1, :, 2 * ch:].reshape(cells, ch)],
            axis=1,
        )
        both = jnp.dot(left, pair[...], preferred_element_type=F32)
        third = jnp.dot(left[:, 0:last], single[...], preferred_element_type=F32)
        edge = jnp.zeros((rows, ch), F32)
        before = jnp.concatenate([edge, both[0:cells - rows, 0:ch]], axis=0)
        after = jnp.concatenate([third[rows:], edge], axis=0)
        return both[:, ch:] + before + after

    def as_f32(column):
        return column.reshape(cells, ch).astype(F32)

    def forward(q):
        hidden = conv(x3, wv, ww, q) + bias_ref[...]
        sigma = jax.nn.sigmoid(hidden)
        value = (as_f32(upb[q]) * (0.2 + 0.8 * sigma)).astype(BF16)
        if q < cols:
            sig[q] = sigma
            ghp[q, 1:frames + 1] = value.reshape(frames, rows, ch)
        widen(value.astype(F32), h3, q + 1)

    def backward(q):
        value = conv(h3, wt, wu, q)
        if q == cols:
            value = jnp.where(has_outer, value, 0.0)
        if q == 0:
            gs[...] = value.astype(BF16).reshape(frames, rows, ch)
        widen(value.astype(BF16).astype(F32), g3, q + 1)
        return jnp.sum(value * value, axis=0, keepdims=True)

    def curve(q):
        sigma = sig[q]
        value = (conv(g3, wv, ww, q) * as_f32(upb[q]) * (0.8 * sigma * (1.0 - sigma))).astype(BF16)
        cvp[q, 1:frames + 1] = value.reshape(frames, rows, ch)
        return jnp.sum(value.astype(F32), axis=0, keepdims=True)

    for q in range(cols):
        widen(as_f32(xb[q + 1]), x3, q + 1)
    for copy in w_loads + up_loads + [bias_load]:
        copy.wait()
    inner = list(range(1, cols - 1))
    for q in inner:
        forward(q)
    for a in range(3):
        for b in range(3):
            for c in range(3):
                row = wide * (2 - b) + ch * (2 - c)
                if a == 0 and row == last:
                    block_of = wv[3 * wide:, ch:2 * ch]
                elif a == 0:
                    block_of = ww[row:row + ch, :]
                else:
                    block_of = wv[row:row + ch, ch * (2 - a):ch * (3 - a)]
                row = wide * b + ch * c
                if a == 2 and row == last:
                    wt[3 * wide:, ch:2 * ch] = block_of.T
                elif a == 2:
                    wu[row:row + ch, :] = block_of.T
                else:
                    wt[row:row + ch, ch * a:ch * (a + 1)] = block_of.T
    for q in range(cols):
        flip(x3, q + 1, xt)
    x_near.wait_recv()
    widen(as_f32(xb[0]), x3, 0)
    forward(0)
    h_near.start()
    flip(x3, 0, xt)

    when_outer(x_far[0].wait_recv)
    widen(as_f32(xb[cols + 1]), x3, cols + 1)
    forward(cols - 1)
    squares = jnp.zeros((1, ch), F32)
    for q in inner:
        squares = squares + backward(q)
    flip(x3, cols + 1, xt)
    for b in range(3):
        flip_ends(x3, b, xe)
    h_near.wait_recv()
    widen(as_f32(hr[...]), h3, 0)
    squares = squares + backward(0)
    g_near.start()
    when_outer(x_far[1].wait_recv, up_far[0].wait_recv)
    widen(as_f32(xb[cols + 2]), x3, cols + 2)
    forward(cols)
    squares = squares + backward(cols - 1)
    for q in range(cols):
        flip(g3, q + 1, gt)

    units = [((0, 2), b) for b in range(3)] + [((1,), b) for b in range(3)]

    def near(b):
        return [w for w in range(cols) if 1 <= w + b <= cols]

    def columns(pads, lo, hi, a):
        return [pads[lo:hi, 2 - a:2 - a + main].reshape((hi - lo) * lanes, ch)]

    def column_ends(pads, a):
        parts = [pads[w, 2 - a + main:2 - a + frames].reshape(spare * rows, ch) for w in range(cols)]
        return parts + [jnp.zeros((xe.shape[2] - ends, ch), BF16)]

    sums = scratch[29] if scatter else out_ref

    def place(a, b):
        return pl.ds(pl.multiple_of(wide * (3 * a + tap_at(b)), ch), wide)

    def terms_near(unit):
        taps, b = unit
        lo, hi = near(b)[0], near(b)[-1] + 1
        right = jnp.concatenate([columns(ghp, lo, hi, a)[0] for a in taps], axis=1)
        value = jnp.dot(gt[:, (lo + b) * lanes:(hi + b) * lanes], right, preferred_element_type=F32)
        for n, a in enumerate(taps):
            sums[place(a, b), :] = value[:, n * ch:(n + 1) * ch]

    def terms_rest(unit):
        taps, b = unit
        far = [w for w in range(cols) if w not in near(b)]
        left = jnp.concatenate(
            [xt[:, b * lanes:(b + cols) * lanes]]
            + [gt[:, (w + b) * lanes:(w + b + 1) * lanes] for w in far]
            + [xe[b], ge[b]],
            axis=1,
        )
        right = jnp.concatenate(
            [
                jnp.concatenate(
                    columns(cvp, 0, cols, a)
                    + [part for w in far for part in columns(ghp, w, w + 1, a)]
                    + column_ends(cvp, a)
                    + column_ends(ghp, a),
                    axis=0,
                )
                for a in taps
            ],
            axis=1,
        )
        value = jnp.dot(left, right, preferred_element_type=F32)
        for n, a in enumerate(taps):
            sums[place(a, b), :] = sums[place(a, b), :] + value[:, n * ch:(n + 1) * ch]

    for unit in units:
        terms_near(unit)
    g_near.wait_recv()
    when_outer(x_far[2].wait_recv, up_far[1].wait_recv)
    widen(as_f32(gr[...]), g3, 0)
    widen(as_f32(xb[cols + 3]), x3, cols + 3)
    forward(cols + 1)
    bias_sum = jnp.zeros((1, ch), F32)
    for q in range(cols - 1):
        bias_sum = bias_sum + curve(q)
    backward(cols)
    flip(g3, 0, gt)
    flip(g3, cols + 1, gt)
    for b in range(3):
        flip_ends(g3, b, ge)
    bias_sum = bias_sum + curve(cols - 1)
    st[...] = jnp.zeros_like(st)
    st[0:1, :] = bias_sum
    st[1:2, :] = squares

    if not scatter:
        for unit in units:
            terms_rest(unit)
        stat_ref[...] = st[...]
    else:
        (pf, pr, pb, rb, zb, rz, own, og, qb, rq, qown, qc, sr, s2, sb, sz, pair_send, pair_recv, sc_send,
         sc_recv, z_send, z_recv, ag_send, ag_recv, q_send, q_recv, qc_send, qc_recv, stat_send,
         stat_recv) = scratch[29:]
        half = tiles // 2
        z = t // 2
        thick = clips * piece

        def clip_at(step):
            return lax.rem(k + step, clips)

        def z_at(step):
            return lax.rem(z + step, half)

        def block_at(tile, start, size):
            return pl.ds(pl.multiple_of(tile * block + start, 16), size)

        stat_pair = remote(st, sr, stat_send.at[0], stat_recv.at[0], (k, other))
        stat_clip = [
            remote(s2, sb.at[k], stat_send.at[dk], stat_recv.at[1 + k], (clip_at(dk), t))
            for dk in range(1, clips)
        ]
        stat_z = [
            remote(sb.at[k], sz.at[z], stat_send.at[clips + dz], stat_recv.at[1 + clips + z],
                   (k, 2 * z_at(dz) + core))
            for dz in range(1, half)
        ]

        def stats_a():
            stat_pair.wait_recv()
            s2[...] = st[...] + sr[...]
            for copy in stat_clip:
                copy.start()

        def stats_b():
            total = s2[...]
            for dk in range(1, clips):
                slot = clip_at(dk)
                remote(s2, sb.at[slot], stat_send.at[dk], stat_recv.at[1 + slot], (slot, t)).wait_recv()
                total = total + sb[slot]
            sb[k] = total
            for copy in stat_z:
                copy.start()

        def stats_c():
            total = sb[k]
            for dz in range(1, half):
                slot = z_at(dz)
                remote(
                    sb.at[k], sz.at[slot], stat_send.at[clips + dz], stat_recv.at[1 + clips + slot],
                    (k, 2 * slot + core),
                ).wait_recv()
                total = total + sz[slot]
            bias_out[...] = factor * total[0:1, :]
            pen_ref[...] = 0.5 * factor * jnp.sum(total[1:2, :], axis=1, keepdims=True)

        stat_pair.start()

        def ready(j):
            lo, hi = 2 * j * block, (2 * j + 2) * block
            return set(range(lo // wide, (hi - 1) // wide + 1))

        pairs = [
            remote(pf.at[block_at(2 * j + 1 - core, 0, block)], pr.at[j], pair_send.at[j], pair_recv.at[j],
                   (k, other))
            for j in range(half)
        ]
        clip_sends = [
            [
                remote(pb.at[j, clip_at(dk)], rb.at[j, k], sc_send.at[j, dk], sc_recv.at[j, k],
                       (clip_at(dk), t))
                for dk in range(1, clips)
            ]
            for j in range(half)
        ]
        z_sends = [
            remote(zb.at[j], rz.at[z], z_send.at[j], z_recv.at[z], (k, 2 * j + core)) for j in range(half)
        ]
        q_sends = [
            remote(qb.at[j], rq.at[z], q_send.at[j], q_recv.at[z], (k, 2 * j + core)) for j in range(half)
        ]

        def after_pair(j):
            pairs[j].wait_recv()
            first = pf[block_at(2 * j + core, 0, thick), :] + pr[j, 0:thick]
            pf[block_at(2 * j + core, 0, thick), :] = first
            pb[j] = first.astype(BF16).reshape(clips, piece, ch)
            for copy in clip_sends[j]:
                copy.start()
            second = pf[block_at(2 * j + core, thick, block - thick), :] + pr[j, thick:block]

            @pl.when(z == j)
            def _():
                qown[...] = second

            @pl.when(z != j)
            def _():
                qb[j] = second.astype(BF16)
                q_sends[j].start()

        def over_z(j):
            total = pf[block_at(2 * j + core, k * piece, piece), :]
            for dk in range(1, clips):
                slot = clip_at(dk)
                remote(pb.at[j, slot], rb.at[j, slot], sc_send.at[j, dk], sc_recv.at[j, slot],
                       (slot, t)).wait_recv()
                total = total + rb[j, slot].astype(F32)

            @pl.when(z == j)
            def _():
                own[...] = total

            @pl.when(z != j)
            def _():
                zb[j] = total.astype(BF16)
                z_sends[j].start()

        done, begun, paired = (set(), set()), [], []
        for n, part in enumerate((units[:3], units[3:])):
            for unit in part:
                terms_rest(unit)
                for a in unit[0]:
                    done[0].add(3 * a + unit[1])
                    done[1].add(3 * a + 2 - unit[1])
            fresh = [j for j in range(half) if j not in begun and ready(j) <= done[0] & done[1]]
            for j in fresh:
                pairs[j].start()
            if n == 0:
                stats_a()
            for j in paired:
                after_pair(j)
            begun += fresh
            paired = fresh
        for j in paired:
            after_pair(j)
        stats_b()
        for j in begun:
            over_z(j)

        total = qown[...]
        for dz in range(1, half):
            slot = z_at(dz)
            remote(qb.at[0], rq.at[slot], q_send.at[0], q_recv.at[slot], (k, 2 * slot + core)).wait_recv()
            total = total + rq[slot].astype(F32)
        qc[k] = total.astype(BF16)
        spreads = [
            remote(qc.at[k], qc.at[k], qc_send.at[dk], qc_recv.at[k], (clip_at(dk), t))
            for dk in range(1, clips)
        ]
        for copy in spreads:
            copy.start()

        total = own[...]
        for dz in range(1, half):
            slot = z_at(dz)
            remote(zb.at[0], rz.at[slot], z_send.at[0], z_recv.at[slot], (k, 2 * slot + core)).wait_recv()
            total = total + rz[slot].astype(F32)
        og[k] = factor * total
        gathers = [
            remote(og.at[k], og.at[k], ag_send.at[dk], ag_recv.at[k], (clip_at(dk), t))
            for dk in range(1, clips)
        ]
        for copy in gathers:
            copy.start()
        stats_c()
        for dk in range(1, clips):
            slot = clip_at(dk)
            remote(qc.at[slot], qc.at[slot], qc_send.at[dk], qc_recv.at[slot], (slot, t)).wait_recv()
        total = qc[0].astype(F32)
        for slot in range(1, clips):
            total = total + qc[slot].astype(F32)
        out_ref[thick:block, :] = factor * total
        for dk in range(1, clips):
            slot = clip_at(dk)
            remote(og.at[slot], og.at[slot], ag_send.at[dk], ag_recv.at[slot], (slot, t)).wait_recv()
        out_ref[0:thick, :] = og[...].reshape(thick, ch)
        for copy in gathers + spreads + stat_clip + stat_z + [stat_pair] + pairs:
            copy.wait_send()
        for j in range(half):
            for copy in clip_sends[j]:
                copy.wait_send()

            @pl.when(z != j)
            def _():
                z_sends[j].wait_send()
                q_sends[j].wait_send()
    for copy in (x_near, h_near, g_near):
        copy.wait_send()
    when_outer(*[copy.wait_send for copy in x_far + up_far])


def shards(clip_features, upstream, weight, conv_bias):
    count, frames, cols, rows, ch = clip_features.shape
    clips = lax.axis_size("clip")
    tiles = lax.axis_size("tile")
    factor = r1_weight / (count * clips * frames * rows * cols * tiles)
    weight_rows = weight.shape[0] * ch
    block = weight_rows // tiles
    scatter = block % 16 == 0
    piece = max(1, block * SHARE // (1600 * clips)) * 16
    wide = 3 * ch
    main = frames - frames % (128 // rows)
    ends = -(-cols * (frames - main) * rows // 128) * 128
    geo = (clips, tiles, frames, cols, rows, ch, block, piece, scatter, factor)
    dma = pltpu.SemaphoreType.DMA

    def field(width):
        return pltpu.VMEM((width, frames + 1, rows, wide), BF16)

    flipped = pltpu.VMEM((wide, (cols + 2) * main * rows), BF16)
    flipped_ends = pltpu.VMEM((3, wide, ends), BF16)
    thin = pltpu.VMEM((cols, frames + 2, rows, ch), BF16)
    pair, single = pltpu.VMEM((10 * ch, 2 * ch), BF16), pltpu.VMEM((8 * ch, ch), BF16)
    edge = pltpu.VMEM((frames, rows, ch), BF16)
    scratch = [
        pltpu.VMEM((1, ch), F32),
        pltpu.VMEM((cols + 4, frames, rows, ch), BF16),
        pltpu.VMEM((cols + 2, frames, rows, ch), BF16),
        pair, single, pair, single,
        field(cols + 4), field(cols + 3), field(cols + 2), flipped, flipped, flipped_ends, flipped_ends,
        thin, thin,
        pltpu.VMEM((cols, frames * rows, ch), F32),
        edge, edge, edge,
        pltpu.VMEM((8, ch), F32),
        dma, dma((cols,)), dma((cols,)), dma((10,)), dma((3,)), dma((3,)), dma((5,)), dma((5,)),
    ]
    half = tiles // 2
    out_rows = weight_rows
    if scatter:
        out_rows = block
        others = block - clips * piece
        scratch += [
            pltpu.VMEM((weight_rows, ch), F32),
            pltpu.VMEM((half, block, ch), F32),
            pltpu.VMEM((half, clips, piece, ch), BF16),
            pltpu.VMEM((half, clips, piece, ch), BF16),
            pltpu.VMEM((half, piece, ch), BF16),
            pltpu.VMEM((half, piece, ch), BF16),
            pltpu.VMEM((piece, ch), F32),
            pltpu.VMEM((clips, piece, ch), F32),
            pltpu.VMEM((half, others, ch), BF16),
            pltpu.VMEM((half, others, ch), BF16),
            pltpu.VMEM((others, ch), F32),
            pltpu.VMEM((clips, others, ch), BF16),
            pltpu.VMEM((8, ch), F32),
            pltpu.VMEM((8, ch), F32),
            pltpu.VMEM((clips, 8, ch), F32),
            pltpu.VMEM((half, 8, ch), F32),
            dma((half,)), dma((half,)), dma((half, clips)), dma((half, clips)),
            dma((half,)), dma((half,)), dma((clips,)), dma((clips,)),
            dma((half,)), dma((half,)), dma((clips,)), dma((clips,)),
            dma((clips + half,)), dma((1 + clips + half,)),
        ]
    hbm = pl.BlockSpec(memory_space=pltpu.HBM)
    vmem = pl.BlockSpec(memory_space=pltpu.VMEM)
    outs = (jax.ShapeDtypeStruct((out_rows, ch), F32), jax.ShapeDtypeStruct((8, ch), F32))
    if scatter:
        outs = (pltpu.VMEM((out_rows, ch), F32), pltpu.VMEM((1, ch), F32), jax.ShapeDtypeStruct((1, 1), F32))
    results = pl.pallas_call(
        functools.partial(kernel, geo),
        out_shape=outs,
        in_specs=[hbm, hbm, hbm, hbm],
        out_specs=(vmem,) * len(outs),
        scratch_shapes=scratch,
        compiler_params=pltpu.CompilerParams(
            collective_id=0, has_side_effects=True, vmem_limit_bytes=60 * 1024 * 1024
        ),
        name="r1_section",
    )(
        clip_features.reshape(frames, cols, rows, ch),
        upstream.reshape(frames, cols, rows, ch),
        weight.reshape(9, wide, ch),
        conv_bias.reshape(1, ch),
    )
    if scatter:
        return results[0], results[1].reshape(ch), results[2].reshape(())
    grads, stats = results
    grads = factor * lax.psum(lax.psum_scatter(grads, "tile", scatter_dimension=0, tiled=True), "clip")
    stats = lax.psum(stats, ("clip", "tile"))
    return grads, factor * stats[0], 0.5 * factor * jnp.sum(stats[1])


def solution(mesh):
    in_specs = (P("clip", None, "tile", None, None), P("clip", None, "tile", None, None), P(), P())
    out_specs = (P("tile", None), P(), P())
    return jax.shard_map(shards, mesh=mesh, in_specs=in_specs, out_specs=out_specs, check_vma=False)
```

```python
import functools

import jax
import jax.numpy as jnp
from jax import lax
from jax.experimental import pallas as pl
from jax.experimental.pallas import tpu as pltpu
from jax.sharding import PartitionSpec as P

r1_weight = 10.0
MESH = pl.DeviceIdType.MESH
BF16 = jnp.bfloat16
F32 = jnp.float32
SHARE = 75


def kernel(geo, x_hbm, up_hbm, w_hbm, bias_hbm, out_ref, *rest):
    (clips, tiles, frames, cols, rows, ch, block, piece, scatter, factor) = geo
    if scatter:
        bias_out, pen_ref, *scratch = rest
    else:
        stat_ref, *scratch = rest
    (kept_x, kept_h, bias_ref, xb, upb, wv, ww, wt, wu, x3, h3, g3, xt, gt, xe, ge, ghp, cvp, sig, hr, hf, gs, gr, st,
     bias_sem, load_sem, up_sem, w_sem, near_send, near_recv, far_send, far_recv) = scratch[:32]
    k = lax.axis_index("clip")
    t = lax.axis_index("tile")
    core = lax.rem(t, 2)
    other = t + 1 - 2 * core
    outer = t - 1 + 2 * core
    has_outer = jnp.logical_and(outer >= 0, outer < tiles)
    outer_at = (k, jnp.clip(outer, 0, tiles - 1))
    cells = frames * rows
    wide = 3 * ch
    last = 9 * ch - ch
    main = xt.shape[1] // ((cols + 2) * rows)
    lanes = main * rows

    def column_at(q):
        return cols - 1 - q + core * (2 * q - cols + 1)

    def tap_at(b):
        return 2 - b + core * (2 * b - 2)

    peers = [(0, dt) for dt in (1, tiles - 1)] + [(dk, 0) for dk in range(1, clips)]
    peers += [(0, dt) for dt in range(2, tiles - 1)]
    barrier = pltpu.get_barrier_semaphore()
    if scatter:
        for dk, dt in peers:
            pl.semaphore_signal(
                barrier, inc=1,
                device_id=(lax.rem(k + dk, clips), lax.rem(t + dt, tiles)), device_id_type=MESH,
            )
    else:
        for step in (1, tiles - 1):
            pl.semaphore_signal(
                barrier, inc=1, device_id=(k, lax.rem(t + step, tiles)), device_id_type=MESH
            )

    x_loads = [
        pltpu.make_async_copy(x_hbm.at[:, column_at(q)], xb.at[q + 1], load_sem.at[q]) for q in range(cols)
    ]
    for copy in x_loads:
        copy.start()
    w_loads = [
        pltpu.make_async_copy(
            w_hbm.at[3 * a + tap_at(b)], wv.at[wide * b:wide * (b + 1), a * ch:(a + 1) * ch],
            w_sem.at[3 * a + b],
        )
        for a in range(2)
        for b in range(3)
    ]
    w_loads += [
        pltpu.make_async_copy(w_hbm.at[6 + tap_at(b)], ww.at[wide * b:wide * (b + 1)], w_sem.at[6 + b])
        for b in range(2)
    ]
    w_loads += [
        pltpu.make_async_copy(w_hbm.at[6 + tap_at(2), 0:2 * ch], ww.at[2 * wide:last], w_sem.at[8]),
        pltpu.make_async_copy(
            w_hbm.at[6 + tap_at(2), 2 * ch:wide], wv.at[3 * wide:3 * wide + ch, ch:2 * ch], w_sem.at[9]
        ),
    ]
    for copy in w_loads:
        copy.start()
    up_loads = [
        pltpu.make_async_copy(up_hbm.at[:, column_at(q)], upb.at[q], up_sem.at[q]) for q in range(cols)
    ]
    for copy in up_loads:
        copy.start()
    bias_load = pltpu.make_async_copy(bias_hbm, bias_ref, bias_sem)
    bias_load.start()

    def remote(src, dst, send_sem, recv_sem, device):
        return pltpu.make_async_remote_copy(
            src_ref=src, dst_ref=dst, send_sem=send_sem, recv_sem=recv_sem,
            device_id=device, device_id_type=MESH,
        )

    def to_other(n, src, dst):
        return remote(src, dst, near_send.at[n], near_recv.at[n], (k, other))

    def to_outer(n, src, dst):
        return remote(src, dst, far_send.at[n], far_recv.at[n], outer_at)

    x_near = to_other(0, xb.at[1], xb.at[0])
    h_near = to_other(1, ghp.at[0, 1:frames + 1], hr)
    g_near = to_other(2, gs, gr)
    x_far = [to_outer(i, xb.at[cols - i], xb.at[cols + 1 + i]) for i in range(2)]
    up_far = to_outer(2, up_hbm.at[:, column_at(cols - 1)], upb.at[cols])
    h_far = to_outer(3, ghp.at[cols - 2, 1:frames + 1], hf)

    def when_outer(*steps):
        @pl.when(has_outer)
        def _():
            for step in steps:
                step()

    if scatter:
        pl.semaphore_wait(barrier, len(peers))
    else:
        pl.semaphore_wait(barrier, 2)
    for copy in x_loads:
        copy.wait()
    x_near.start()
    when_outer(x_far[0].start, x_far[1].start, up_far.start)

    zero_wide = jnp.zeros((rows, wide), BF16)
    for field in (x3, h3, g3):
        for w in range(field.shape[0]):
            field[w, frames] = zero_wide
    zero_thin = jnp.zeros((rows, ch), BF16)
    for field in (ghp, cvp):
        for w in range(cols):
            for f in (0, frames + 1):
                field[w, f] = zero_thin
    for field in (wv, wt):
        field[3 * wide:, 0:ch] = jnp.zeros((ch, ch), BF16)
    zero_col = jnp.zeros((frames, rows, ch), BF16)

    @pl.when(jnp.logical_not(has_outer))
    def _():
        for i in range(2):
            xb[cols + 1 + i] = zero_col
        upb[cols] = zero_col
        hf[...] = zero_col

    row_at = lax.rem(lax.broadcasted_iota(jnp.int32, (cells, ch), 0), rows)
    first_row = row_at == 0
    last_row = row_at == rows - 1

    def widen(value, field, w):
        before = jnp.where(first_row, 0.0, pltpu.roll(value, 1, 0)).astype(BF16)
        after = jnp.where(last_row, 0.0, pltpu.roll(value, cells - 1, 0)).astype(BF16)
        shape = (frames, rows, ch)
        field[w, 0:frames, :, 0:ch] = before.reshape(shape)
        field[w, 0:frames, :, ch:2 * ch] = value.astype(BF16).reshape(shape)
        field[w, 0:frames, :, 2 * ch:] = after.reshape(shape)

    def flip(field, w, target):
        target[:, w * lanes:(w + 1) * lanes] = field[w, 0:main].reshape(lanes, wide).T

    spare = frames - main
    ends = cols * spare * rows

    def flip_ends(field, b, target):
        parts = [field[w + b, main:frames].reshape(spare * rows, wide) for w in range(cols)]
        parts.append(jnp.zeros((target.shape[2] - ends, wide), BF16))
        target[b] = jnp.concatenate(parts, axis=0).T

    def shifted(both, third):
        edge = jnp.zeros((rows, ch), F32)
        before = jnp.concatenate([edge, both[0:cells - rows, 0:ch]], axis=0)
        after = jnp.concatenate([third[rows:], edge], axis=0)
        return both[:, ch:] + before + after

    def across(field, q, lo, hi):
        return [field[q + b, 0:frames].reshape(cells, wide) for b in range(lo, hi)]

    def ahead(field, q):
        return field[q + 2, 1:frames + 1, :, 2 * ch:].reshape(cells, ch)

    def conv(field, pair, single, q):
        left = jnp.concatenate(across(field, q, 0, 3) + [ahead(field, q)], axis=1)
        both = jnp.dot(left, pair[...], preferred_element_type=F32)
        third = jnp.dot(left[:, 0:last], single[...], preferred_element_type=F32)
        return shifted(both, third)

    def conv_early(field, pair, single, q, kept):
        left = jnp.concatenate(across(field, q, 0, 2), axis=1)
        both = jnp.dot(left, pair[0:2 * wide], preferred_element_type=F32)
        third = jnp.dot(left, single[0:2 * wide], preferred_element_type=F32)
        kept[...] = shifted(both, third)

    def conv_late(field, pair, single, q, kept):
        left = jnp.concatenate(across(field, q, 2, 3) + [ahead(field, q)], axis=1)
        both = jnp.dot(left, pair[2 * wide:], preferred_element_type=F32)
        third = jnp.dot(left[:, 0:last - 2 * wide], single[2 * wide:], preferred_element_type=F32)
        return kept[...] + shifted(both, third)

    def as_f32(column):
        return column.reshape(cells, ch).astype(F32)

    def forward(q, kept=None):
        hidden = (conv_late(x3, wv, ww, q, kept) if kept is not None else conv(x3, wv, ww, q)) + bias_ref[...]
        if q == cols:
            when_outer(up_far.wait_recv)
        sigma = jax.nn.sigmoid(hidden)
        value = (as_f32(upb[q]) * (0.2 + 0.8 * sigma)).astype(BF16)
        if q < cols:
            sig[q] = sigma
            ghp[q, 1:frames + 1] = value.reshape(frames, rows, ch)
        widen(value.astype(F32), h3, q + 1)

    def backward(q, kept=None):
        value = conv_late(h3, wt, wu, q, kept) if kept is not None else conv(h3, wt, wu, q)
        if q == cols:
            value = jnp.where(has_outer, value, 0.0)
        if q == 0:
            gs[...] = value.astype(BF16).reshape(frames, rows, ch)
        widen(value.astype(BF16).astype(F32), g3, q + 1)
        return jnp.sum(value * value, axis=0, keepdims=True)

    def curve(q):
        sigma = sig[q]
        value = (conv(g3, wv, ww, q) * as_f32(upb[q]) * (0.8 * sigma * (1.0 - sigma))).astype(BF16)
        cvp[q, 1:frames + 1] = value.reshape(frames, rows, ch)
        return jnp.sum(value.astype(F32), axis=0, keepdims=True)

    for q in range(cols):
        widen(as_f32(xb[q + 1]), x3, q + 1)
    for copy in w_loads + up_loads + [bias_load]:
        copy.wait()
    inner = list(range(1, cols - 1))
    for q in inner:
        forward(q)
    when_outer(h_far.start)
    for a in range(3):
        for b in range(3):
            for c in range(3):
                row = wide * (2 - b) + ch * (2 - c)
                if a == 0 and row == last:
                    block_of = wv[3 * wide:, ch:2 * ch]
                elif a == 0:
                    block_of = ww[row:row + ch, :]
                else:
                    block_of = wv[row:row + ch, ch * (2 - a):ch * (3 - a)]
                row = wide * b + ch * c
                if a == 2 and row == last:
                    wt[3 * wide:, ch:2 * ch] = block_of.T
                elif a == 2:
                    wu[row:row + ch, :] = block_of.T
                else:
                    wt[row:row + ch, ch * a:ch * (a + 1)] = block_of.T
    conv_early(x3, wv, ww, cols - 1, kept_x)
    x_near.wait_recv()
    widen(as_f32(xb[0]), x3, 0)
    forward(0)
    h_near.start()
    for q in range(-1, cols):
        flip(x3, q + 1, xt)
    flip_ends(x3, 0, xe)
    flip_ends(x3, 1, xe)
    conv_early(h3, wt, wu, cols - 2, kept_h)
    h_near.wait_recv()
    widen(as_f32(hr[...]), h3, 0)
    squares = backward(0)
    g_near.start()

    when_outer(x_far[0].wait_recv)
    widen(as_f32(xb[cols + 1]), x3, cols + 1)
    forward(cols - 1, kept_x)
    for q in inner:
        squares = squares + backward(q, kept_h if q == cols - 2 else None)
    flip(x3, cols + 1, xt)
    flip_ends(x3, 2, xe)
    when_outer(x_far[1].wait_recv)
    widen(as_f32(xb[cols + 2]), x3, cols + 2)
    forward(cols)
    squares = squares + backward(cols - 1)
    for q in range(cols):
        flip(g3, q + 1, gt)

    units = [((0, 2), b) for b in range(3)] + [((1,), b) for b in range(3)]

    def near(b):
        return [w for w in range(cols) if 1 <= w + b <= cols]

    def columns(pads, lo, hi, a):
        return [pads[lo:hi, 2 - a:2 - a + main].reshape((hi - lo) * lanes, ch)]

    def column_ends(pads, a):
        parts = [pads[w, 2 - a + main:2 - a + frames].reshape(spare * rows, ch) for w in range(cols)]
        return parts + [jnp.zeros((xe.shape[2] - ends, ch), BF16)]

    sums = scratch[32] if scatter else out_ref

    def place(a, b):
        return pl.ds(pl.multiple_of(wide * (3 * a + tap_at(b)), ch), wide)

    def terms_near(unit):
        taps, b = unit
        lo, hi = near(b)[0], near(b)[-1] + 1
        right = jnp.concatenate([columns(ghp, lo, hi, a)[0] for a in taps], axis=1)
        value = jnp.dot(gt[:, (lo + b) * lanes:(hi + b) * lanes], right, preferred_element_type=F32)
        for n, a in enumerate(taps):
            sums[place(a, b), :] = value[:, n * ch:(n + 1) * ch]

    def terms_rest(unit):
        taps, b = unit
        far = [w for w in range(cols) if w not in near(b)]
        left = jnp.concatenate(
            [xt[:, b * lanes:(b + cols) * lanes]]
            + [gt[:, (w + b) * lanes:(w + b + 1) * lanes] for w in far]
            + [xe[b], ge[b]],
            axis=1,
        )
        right = jnp.concatenate(
            [
                jnp.concatenate(
                    columns(cvp, 0, cols, a)
                    + [part for w in far for part in columns(ghp, w, w + 1, a)]
                    + column_ends(cvp, a)
                    + column_ends(ghp, a),
                    axis=0,
                )
                for a in taps
            ],
            axis=1,
        )
        value = jnp.dot(left, right, preferred_element_type=F32)
        for n, a in enumerate(taps):
            sums[place(a, b), :] = sums[place(a, b), :] + value[:, n * ch:(n + 1) * ch]

    for unit in units:
        terms_near(unit)
    g_near.wait_recv()
    when_outer(h_far.wait_recv)
    widen(as_f32(gr[...]), g3, 0)
    widen(as_f32(hf[...]), h3, cols + 2)
    bias_sum = jnp.zeros((1, ch), F32)
    for q in range(cols - 1):
        bias_sum = bias_sum + curve(q)
    backward(cols)
    flip(g3, 0, gt)
    flip(g3, cols + 1, gt)
    for b in range(3):
        flip_ends(g3, b, ge)
    bias_sum = bias_sum + curve(cols - 1)
    st[...] = jnp.zeros_like(st)
    st[0:1, :] = bias_sum
    st[1:2, :] = squares

    if not scatter:
        for unit in units:
            terms_rest(unit)
        stat_ref[...] = st[...]
    else:
        (pf, pr, pb, rb, zb, rz, own, og, qb, rq, qown, qc, sr, s2, sb, sz, pair_send, pair_recv, sc_send,
         sc_recv, z_send, z_recv, ag_send, ag_recv, q_send, q_recv, qc_send, qc_recv, stat_send,
         stat_recv) = scratch[32:]
        half = tiles // 2
        z = t // 2
        thick = clips * piece

        def clip_at(step):
            return lax.rem(k + step, clips)

        def z_at(step):
            return lax.rem(z + step, half)

        def block_at(tile, start, size):
            return pl.ds(pl.multiple_of(tile * block + start, 16), size)

        stat_pair = remote(st, sr, stat_send.at[0], stat_recv.at[0], (k, other))
        stat_clip = [
            remote(s2, sb.at[k], stat_send.at[dk], stat_recv.at[1 + k], (clip_at(dk), t))
            for dk in range(1, clips)
        ]
        stat_z = [
            remote(sb.at[k], sz.at[z], stat_send.at[clips + dz], stat_recv.at[1 + clips + z],
                   (k, 2 * z_at(dz) + core))
            for dz in range(1, half)
        ]

        def stats_a():
            stat_pair.wait_recv()
            s2[...] = st[...] + sr[...]
            for copy in stat_clip:
                copy.start()

        def stats_b():
            total = s2[...]
            for dk in range(1, clips):
                slot = clip_at(dk)
                remote(s2, sb.at[slot], stat_send.at[dk], stat_recv.at[1 + slot], (slot, t)).wait_recv()
                total = total + sb[slot]
            sb[k] = total
            for copy in stat_z:
                copy.start()

        def stats_c():
            total = sb[k]
            for dz in range(1, half):
                slot = z_at(dz)
                remote(
                    sb.at[k], sz.at[slot], stat_send.at[clips + dz], stat_recv.at[1 + clips + slot],
                    (k, 2 * slot + core),
                ).wait_recv()
                total = total + sz[slot]
            bias_out[...] = factor * total[0:1, :]
            pen_ref[...] = 0.5 * factor * jnp.sum(total[1:2, :], axis=1, keepdims=True)

        stat_pair.start()

        def ready(j):
            lo, hi = 2 * j * block, (2 * j + 2) * block
            return set(range(lo // wide, (hi - 1) // wide + 1))

        pairs = [
            remote(pf.at[block_at(2 * j + 1 - core, 0, block)], pr.at[j], pair_send.at[j], pair_recv.at[j],
                   (k, other))
            for j in range(half)
        ]
        clip_sends = [
            [
                remote(pb.at[j, clip_at(dk)], rb.at[j, k], sc_send.at[j, dk], sc_recv.at[j, k],
                       (clip_at(dk), t))
                for dk in range(1, clips)
            ]
            for j in range(half)
        ]
        z_sends = [
            remote(zb.at[j], rz.at[z], z_send.at[j], z_recv.at[z], (k, 2 * j + core)) for j in range(half)
        ]
        q_sends = [
            remote(qb.at[j], rq.at[z], q_send.at[j], q_recv.at[z], (k, 2 * j + core)) for j in range(half)
        ]

        def after_pair(j):
            pairs[j].wait_recv()
            first = pf[block_at(2 * j + core, 0, thick), :] + pr[j, 0:thick]
            pf[block_at(2 * j + core, 0, thick), :] = first
            pb[j] = first.astype(BF16).reshape(clips, piece, ch)
            for copy in clip_sends[j]:
                copy.start()
            second = pf[block_at(2 * j + core, thick, block - thick), :] + pr[j, thick:block]

            @pl.when(z == j)
            def _():
                qown[...] = second

            @pl.when(z != j)
            def _():
                qb[j] = second.astype(BF16)
                q_sends[j].start()

        def over_z(j):
            total = pf[block_at(2 * j + core, k * piece, piece), :]
            for dk in range(1, clips):
                slot = clip_at(dk)
                remote(pb.at[j, slot], rb.at[j, slot], sc_send.at[j, dk], sc_recv.at[j, slot],
                       (slot, t)).wait_recv()
                total = total + rb[j, slot].astype(F32)

            @pl.when(z == j)
            def _():
                own[...] = total

            @pl.when(z != j)
            def _():
                zb[j] = total.astype(BF16)
                z_sends[j].start()

        done, begun, paired = (set(), set()), [], []
        for n, part in enumerate((units[:3], units[3:])):
            for unit in part:
                terms_rest(unit)
                for a in unit[0]:
                    done[0].add(3 * a + unit[1])
                    done[1].add(3 * a + 2 - unit[1])
            fresh = [j for j in range(half) if j not in begun and ready(j) <= done[0] & done[1]]
            for j in fresh:
                pairs[j].start()
            if n == 0:
                stats_a()
            for j in paired:
                after_pair(j)
            begun += fresh
            paired = fresh
        for j in paired:
            after_pair(j)
        stats_b()
        for j in begun:
            over_z(j)

        total = qown[...]
        for dz in range(1, half):
            slot = z_at(dz)
            remote(qb.at[0], rq.at[slot], q_send.at[0], q_recv.at[slot], (k, 2 * slot + core)).wait_recv()
            total = total + rq[slot].astype(F32)
        qc[k] = total.astype(BF16)
        spreads = [
            remote(qc.at[k], qc.at[k], qc_send.at[dk], qc_recv.at[k], (clip_at(dk), t))
            for dk in range(1, clips)
        ]
        for copy in spreads:
            copy.start()

        total = own[...]
        for dz in range(1, half):
            slot = z_at(dz)
            remote(zb.at[0], rz.at[slot], z_send.at[0], z_recv.at[slot], (k, 2 * slot + core)).wait_recv()
            total = total + rz[slot].astype(F32)
        og[k] = factor * total
        gathers = [
            remote(og.at[k], og.at[k], ag_send.at[dk], ag_recv.at[k], (clip_at(dk), t))
            for dk in range(1, clips)
        ]
        for copy in gathers:
            copy.start()
        stats_c()
        for dk in range(1, clips):
            slot = clip_at(dk)
            remote(qc.at[slot], qc.at[slot], qc_send.at[dk], qc_recv.at[slot], (slot, t)).wait_recv()
        total = qc[0].astype(F32)
        for slot in range(1, clips):
            total = total + qc[slot].astype(F32)
        out_ref[thick:block, :] = factor * total
        for dk in range(1, clips):
            slot = clip_at(dk)
            remote(og.at[slot], og.at[slot], ag_send.at[dk], ag_recv.at[slot], (slot, t)).wait_recv()
        out_ref[0:thick, :] = og[...].reshape(thick, ch)
        for copy in gathers + spreads + stat_clip + stat_z + [stat_pair] + pairs:
            copy.wait_send()
        for j in range(half):
            for copy in clip_sends[j]:
                copy.wait_send()

            @pl.when(z != j)
            def _():
                z_sends[j].wait_send()
                q_sends[j].wait_send()
    for copy in (x_near, h_near, g_near):
        copy.wait_send()
    when_outer(*[copy.wait_send for copy in x_far + [up_far, h_far]])


def shards(clip_features, upstream, weight, conv_bias):
    count, frames, cols, rows, ch = clip_features.shape
    clips = lax.axis_size("clip")
    tiles = lax.axis_size("tile")
    factor = r1_weight / (count * clips * frames * rows * cols * tiles)
    weight_rows = weight.shape[0] * ch
    block = weight_rows // tiles
    scatter = block % 16 == 0
    piece = max(1, block * SHARE // (1600 * clips)) * 16
    wide = 3 * ch
    main = frames - frames % (128 // rows)
    ends = -(-cols * (frames - main) * rows // 128) * 128
    geo = (clips, tiles, frames, cols, rows, ch, block, piece, scatter, factor)
    dma = pltpu.SemaphoreType.DMA

    def field(width):
        return pltpu.VMEM((width, frames + 1, rows, wide), BF16)

    flipped = pltpu.VMEM((wide, (cols + 2) * main * rows), BF16)
    flipped_ends = pltpu.VMEM((3, wide, ends), BF16)
    thin = pltpu.VMEM((cols, frames + 2, rows, ch), BF16)
    pair, single = pltpu.VMEM((10 * ch, 2 * ch), BF16), pltpu.VMEM((8 * ch, ch), BF16)
    edge = pltpu.VMEM((frames, rows, ch), BF16)
    scratch = [
        pltpu.VMEM((frames * rows, ch), F32),
        pltpu.VMEM((frames * rows, ch), F32),
        pltpu.VMEM((1, ch), F32),
        pltpu.VMEM((cols + 3, frames, rows, ch), BF16),
        pltpu.VMEM((cols + 1, frames, rows, ch), BF16),
        pair, single, pair, single,
        field(cols + 3), field(cols + 3), field(cols + 2), flipped, flipped, flipped_ends, flipped_ends,
        thin, thin,
        pltpu.VMEM((cols, frames * rows, ch), F32),
        edge, edge, edge, edge,
        pltpu.VMEM((8, ch), F32),
        dma, dma((cols,)), dma((cols,)), dma((10,)), dma((3,)), dma((3,)), dma((4,)), dma((4,)),
    ]
    half = tiles // 2
    out_rows = weight_rows
    if scatter:
        out_rows = block
        others = block - clips * piece
        scratch += [
            pltpu.VMEM((weight_rows, ch), F32),
            pltpu.VMEM((half, block, ch), F32),
            pltpu.VMEM((half, clips, piece, ch), BF16),
            pltpu.VMEM((half, clips, piece, ch), BF16),
            pltpu.VMEM((half, piece, ch), BF16),
            pltpu.VMEM((half, piece, ch), BF16),
            pltpu.VMEM((piece, ch), F32),
            pltpu.VMEM((clips, piece, ch), F32),
            pltpu.VMEM((half, others, ch), BF16),
            pltpu.VMEM((half, others, ch), BF16),
            pltpu.VMEM((others, ch), F32),
            pltpu.VMEM((clips, others, ch), BF16),
            pltpu.VMEM((8, ch), F32),
            pltpu.VMEM((8, ch), F32),
            pltpu.VMEM((clips, 8, ch), F32),
            pltpu.VMEM((half, 8, ch), F32),
            dma((half,)), dma((half,)), dma((half, clips)), dma((half, clips)),
            dma((half,)), dma((half,)), dma((clips,)), dma((clips,)),
            dma((half,)), dma((half,)), dma((clips,)), dma((clips,)),
            dma((clips + half,)), dma((1 + clips + half,)),
        ]
    hbm = pl.BlockSpec(memory_space=pltpu.HBM)
    vmem = pl.BlockSpec(memory_space=pltpu.VMEM)
    outs = (jax.ShapeDtypeStruct((out_rows, ch), F32), jax.ShapeDtypeStruct((8, ch), F32))
    if scatter:
        outs = (pltpu.VMEM((out_rows, ch), F32), pltpu.VMEM((1, ch), F32), jax.ShapeDtypeStruct((1, 1), F32))
    results = pl.pallas_call(
        functools.partial(kernel, geo),
        out_shape=outs,
        in_specs=[hbm, hbm, hbm, hbm],
        out_specs=(vmem,) * len(outs),
        scratch_shapes=scratch,
        compiler_params=pltpu.CompilerParams(
            collective_id=0, has_side_effects=True, vmem_limit_bytes=60 * 1024 * 1024
        ),
        name="r1_section",
    )(
        clip_features.reshape(frames, cols, rows, ch),
        upstream.reshape(frames, cols, rows, ch),
        weight.reshape(9, wide, ch),
        conv_bias.reshape(1, ch),
    )
    if scatter:
        return results[0], results[1].reshape(ch), results[2].reshape(())
    grads, stats = results
    grads = factor * lax.psum(lax.psum_scatter(grads, "tile", scatter_dimension=0, tiled=True), "clip")
    stats = lax.psum(stats, ("clip", "tile"))
    return grads, factor * stats[0], 0.5 * factor * jnp.sum(stats[1])


def solution(mesh):
    in_specs = (P("clip", None, "tile", None, None), P("clip", None, "tile", None, None), P(), P())
    out_specs = (P("tile", None), P(), P())
    return jax.shard_map(shards, mesh=mesh, in_specs=in_specs, out_specs=out_specs, check_vma=False)
```

```python
import functools

import jax
import jax.numpy as jnp
from jax import lax
from jax.experimental import pallas as pl
from jax.experimental.pallas import tpu as pltpu
from jax.sharding import PartitionSpec as P

r1_weight = 10.0
MESH = pl.DeviceIdType.MESH
BF16 = jnp.bfloat16
F32 = jnp.float32
SHARE = 75


def kernel(geo, x_hbm, up_hbm, w_hbm, bias_hbm, out_ref, *rest):
    (clips, tiles, frames, cols, rows, ch, block, piece, scatter, factor) = geo
    if scatter:
        bias_out, pen_ref, *scratch = rest
    else:
        stat_ref, *scratch = rest
    (kept_x, kept_h, bias_ref, xb, upb, wv, ww, wt, wu, x3, h3, g3, xt, gt, xe, ge, ghp, cvp, sig, hr, hf, gs, gr, st,
     bias_sem, load_sem, up_sem, w_sem, near_send, near_recv, far_send, far_recv) = scratch[:32]
    k = lax.axis_index("clip")
    t = lax.axis_index("tile")
    core = lax.rem(t, 2)
    other = t + 1 - 2 * core
    outer = t - 1 + 2 * core
    has_outer = jnp.logical_and(outer >= 0, outer < tiles)
    outer_at = (k, jnp.clip(outer, 0, tiles - 1))
    cells = frames * rows
    wide = 3 * ch
    last = 9 * ch - ch
    main = xt.shape[1] // ((cols + 2) * rows)
    lanes = main * rows

    def column_at(q):
        return cols - 1 - q + core * (2 * q - cols + 1)

    def tap_at(b):
        return 2 - b + core * (2 * b - 2)

    peers = [(0, dt) for dt in (1, tiles - 1)] + [(dk, 0) for dk in range(1, clips)]
    peers += [(0, dt) for dt in range(2, tiles - 1)]
    barrier = pltpu.get_barrier_semaphore()
    if scatter:
        for dk, dt in peers:
            pl.semaphore_signal(
                barrier, inc=1,
                device_id=(lax.rem(k + dk, clips), lax.rem(t + dt, tiles)), device_id_type=MESH,
            )
    else:
        for step in (1, tiles - 1):
            pl.semaphore_signal(
                barrier, inc=1, device_id=(k, lax.rem(t + step, tiles)), device_id_type=MESH
            )

    x_loads = [
        pltpu.make_async_copy(x_hbm.at[:, column_at(q)], xb.at[q + 1], load_sem.at[q]) for q in range(cols)
    ]
    for copy in x_loads:
        copy.start()
    w_loads = [
        pltpu.make_async_copy(
            w_hbm.at[3 * a + tap_at(b)], wv.at[wide * b:wide * (b + 1), a * ch:(a + 1) * ch],
            w_sem.at[3 * a + b],
        )
        for a in range(2)
        for b in range(3)
    ]
    w_loads += [
        pltpu.make_async_copy(w_hbm.at[6 + tap_at(b)], ww.at[wide * b:wide * (b + 1)], w_sem.at[6 + b])
        for b in range(2)
    ]
    w_loads += [
        pltpu.make_async_copy(w_hbm.at[6 + tap_at(2), 0:2 * ch], ww.at[2 * wide:last], w_sem.at[8]),
        pltpu.make_async_copy(
            w_hbm.at[6 + tap_at(2), 2 * ch:wide], wv.at[3 * wide:3 * wide + ch, ch:2 * ch], w_sem.at[9]
        ),
    ]
    for copy in w_loads:
        copy.start()
    up_loads = [
        pltpu.make_async_copy(up_hbm.at[:, column_at(q)], upb.at[q], up_sem.at[q]) for q in range(cols)
    ]
    for copy in up_loads:
        copy.start()
    bias_load = pltpu.make_async_copy(bias_hbm, bias_ref, bias_sem)
    bias_load.start()

    def remote(src, dst, send_sem, recv_sem, device):
        return pltpu.make_async_remote_copy(
            src_ref=src, dst_ref=dst, send_sem=send_sem, recv_sem=recv_sem,
            device_id=device, device_id_type=MESH,
        )

    def to_other(n, src, dst):
        return remote(src, dst, near_send.at[n], near_recv.at[n], (k, other))

    def to_outer(n, src, dst):
        return remote(src, dst, far_send.at[n], far_recv.at[n], outer_at)

    x_near = to_other(0, xb.at[1], xb.at[0])
    h_near = to_other(1, ghp.at[0, 1:frames + 1], hr)
    g_near = to_other(2, gs, gr)
    x_far = [to_outer(i, xb.at[cols - i], xb.at[cols + 1 + i]) for i in range(2)]
    up_far = to_outer(2, up_hbm.at[:, column_at(cols - 1)], upb.at[cols])
    h_far = to_outer(3, ghp.at[cols - 2, 1:frames + 1], hf)

    def when_outer(*steps):
        @pl.when(has_outer)
        def _():
            for step in steps:
                step()

    if scatter:
        pl.semaphore_wait(barrier, len(peers))
    else:
        pl.semaphore_wait(barrier, 2)
    for copy in x_loads:
        copy.wait()
    x_near.start()
    when_outer(x_far[0].start, x_far[1].start, up_far.start)

    zero_wide = jnp.zeros((rows, wide), BF16)
    for field in (x3, h3, g3):
        for w in range(field.shape[0]):
            field[w, frames] = zero_wide
    zero_thin = jnp.zeros((rows, ch), BF16)
    for field in (ghp, cvp):
        for w in range(cols):
            for f in (0, frames + 1):
                field[w, f] = zero_thin
    for field in (wv, wt):
        field[3 * wide:, 0:ch] = jnp.zeros((ch, ch), BF16)
    zero_col = jnp.zeros((frames, rows, ch), BF16)

    @pl.when(jnp.logical_not(has_outer))
    def _():
        for i in range(2):
            xb[cols + 1 + i] = zero_col
        upb[cols] = zero_col
        hf[...] = zero_col

    row_at = lax.rem(lax.broadcasted_iota(jnp.int32, (cells, ch), 0), rows)
    first_row = row_at == 0
    last_row = row_at == rows - 1

    def widen(value, field, w):
        before = jnp.where(first_row, 0.0, pltpu.roll(value, 1, 0)).astype(BF16)
        after = jnp.where(last_row, 0.0, pltpu.roll(value, cells - 1, 0)).astype(BF16)
        shape = (frames, rows, ch)
        field[w, 0:frames, :, 0:ch] = before.reshape(shape)
        field[w, 0:frames, :, ch:2 * ch] = value.astype(BF16).reshape(shape)
        field[w, 0:frames, :, 2 * ch:] = after.reshape(shape)

    def flip(field, w, target):
        target[:, w * lanes:(w + 1) * lanes] = field[w, 0:main].reshape(lanes, wide).T

    spare = frames - main
    ends = (cols + 1) * spare * rows

    def flip_ends(field, n, target):
        parts = [field[w + n, main:frames].reshape(spare * rows, wide) for w in range(cols + 1)]
        if target.shape[2] > ends:
            parts.append(jnp.zeros((target.shape[2] - ends, wide), BF16))
        target[n] = jnp.concatenate(parts, axis=0).T

    def shifted(both, third):
        edge = jnp.zeros((rows, ch), F32)
        before = jnp.concatenate([edge, both[0:cells - rows, 0:ch]], axis=0)
        after = jnp.concatenate([third[rows:], edge], axis=0)
        return both[:, ch:] + before + after

    def across(field, q, lo, hi):
        return [field[q + b, 0:frames].reshape(cells, wide) for b in range(lo, hi)]

    def ahead(field, q):
        return field[q + 2, 1:frames + 1, :, 2 * ch:].reshape(cells, ch)

    def conv(field, pair, single, q):
        left = jnp.concatenate(across(field, q, 0, 3) + [ahead(field, q)], axis=1)
        both = jnp.dot(left, pair[...], preferred_element_type=F32)
        third = jnp.dot(left[:, 0:last], single[...], preferred_element_type=F32)
        return shifted(both, third)

    def conv_early(field, pair, single, q, kept):
        left = jnp.concatenate(across(field, q, 0, 2), axis=1)
        both = jnp.dot(left, pair[0:2 * wide], preferred_element_type=F32)
        third = jnp.dot(left, single[0:2 * wide], preferred_element_type=F32)
        kept[...] = shifted(both, third)

    def conv_late(field, pair, single, q, kept):
        left = jnp.concatenate(across(field, q, 2, 3) + [ahead(field, q)], axis=1)
        both = jnp.dot(left, pair[2 * wide:], preferred_element_type=F32)
        third = jnp.dot(left[:, 0:last - 2 * wide], single[2 * wide:], preferred_element_type=F32)
        return kept[...] + shifted(both, third)

    def as_f32(column):
        return column.reshape(cells, ch).astype(F32)

    def forward(q, kept=None):
        hidden = (conv_late(x3, wv, ww, q, kept) if kept is not None else conv(x3, wv, ww, q)) + bias_ref[...]
        if q == cols:
            when_outer(up_far.wait_recv)
        sigma = jax.nn.sigmoid(hidden)
        value = (as_f32(upb[q]) * (0.2 + 0.8 * sigma)).astype(BF16)
        if q < cols:
            sig[q] = sigma
            ghp[q, 1:frames + 1] = value.reshape(frames, rows, ch)
        widen(value.astype(F32), h3, q + 1)

    def backward(q, kept=None):
        value = conv_late(h3, wt, wu, q, kept) if kept is not None else conv(h3, wt, wu, q)
        if q == cols:
            value = jnp.where(has_outer, value, 0.0)
        if q == 0:
            gs[...] = value.astype(BF16).reshape(frames, rows, ch)
        widen(value.astype(BF16).astype(F32), g3, q + 1)
        return jnp.sum(value * value, axis=0, keepdims=True)

    def curve(q):
        sigma = sig[q]
        value = (conv(g3, wv, ww, q) * as_f32(upb[q]) * (0.8 * sigma * (1.0 - sigma))).astype(BF16)
        cvp[q, 1:frames + 1] = value.reshape(frames, rows, ch)
        return jnp.sum(value.astype(F32), axis=0, keepdims=True)

    for q in range(cols):
        widen(as_f32(xb[q + 1]), x3, q + 1)
    for copy in w_loads + up_loads + [bias_load]:
        copy.wait()
    inner = list(range(1, cols - 1))
    for q in inner:
        forward(q)
    when_outer(h_far.start)
    for a in range(3):
        for b in range(3):
            for c in range(3):
                row = wide * (2 - b) + ch * (2 - c)
                if a == 0 and row == last:
                    block_of = wv[3 * wide:, ch:2 * ch]
                elif a == 0:
                    block_of = ww[row:row + ch, :]
                else:
                    block_of = wv[row:row + ch, ch * (2 - a):ch * (3 - a)]
                row = wide * b + ch * c
                if a == 2 and row == last:
                    wt[3 * wide:, ch:2 * ch] = block_of.T
                elif a == 2:
                    wu[row:row + ch, :] = block_of.T
                else:
                    wt[row:row + ch, ch * a:ch * (a + 1)] = block_of.T
    conv_early(x3, wv, ww, cols - 1, kept_x)
    x_near.wait_recv()
    widen(as_f32(xb[0]), x3, 0)
    forward(0)
    h_near.start()
    for q in range(-1, cols):
        flip(x3, q + 1, xt)
    flip_ends(x3, 0, xe)
    conv_early(h3, wt, wu, cols - 2, kept_h)
    h_near.wait_recv()
    widen(as_f32(hr[...]), h3, 0)
    squares = backward(0)
    g_near.start()

    when_outer(x_far[0].wait_recv)
    widen(as_f32(xb[cols + 1]), x3, cols + 1)
    forward(cols - 1, kept_x)
    for q in inner:
        squares = squares + backward(q, kept_h if q == cols - 2 else None)
    flip(x3, cols + 1, xt)
    flip_ends(x3, 1, xe)
    when_outer(x_far[1].wait_recv)
    widen(as_f32(xb[cols + 2]), x3, cols + 2)
    forward(cols)
    squares = squares + backward(cols - 1)
    for q in range(cols):
        flip(g3, q + 1, gt)

    units = [((0, b), (2, b)) for b in range(3)] + [((1, 0), (1, 1)), ((1, 2),)]

    def factor_of(pads, l, a, b):
        if 0 <= l - b < cols:
            return pads[l - b, 2 - a:2 - a + main].reshape(lanes, ch)
        return jnp.zeros((lanes, ch), BF16)

    def end_factors(pads, n, a, b):
        parts = []
        for w in range(cols + 1):
            if 0 <= w + n - b < cols:
                parts.append(pads[w + n - b, 2 - a + main:2 - a + frames].reshape(spare * rows, ch))
            else:
                parts.append(jnp.zeros((spare * rows, ch), BF16))
        if xe.shape[2] > ends:
            parts.append(jnp.zeros((xe.shape[2] - ends, ch), BF16))
        return parts

    def columns_of(unit):
        return sorted({w + b for _, b in unit for w in range(cols)})

    sums = scratch[32] if scatter else out_ref

    def place(a, b):
        return pl.ds(pl.multiple_of(wide * (3 * a + tap_at(b)), ch), wide)

    def at(l):
        return slice(l * lanes, (l + 1) * lanes)

    def product(left, right):
        left = jnp.concatenate(left, axis=1)
        right = jnp.concatenate([jnp.concatenate(parts, axis=0) for parts in right], axis=1)
        return jnp.dot(left, right, preferred_element_type=F32)

    def terms_near(unit):
        inside = [l for l in columns_of(unit) if 1 <= l <= cols]
        value = product(
            [gt[:, at(l)] for l in inside],
            [[factor_of(ghp, l, a, b) for l in inside] for a, b in unit],
        )
        for n, (a, b) in enumerate(unit):
            sums[place(a, b), :] = value[:, n * ch:(n + 1) * ch]

    def terms_rest(unit):
        ls = columns_of(unit)
        begun_near = unit in units[:3]
        outside = [l for l in ls if not (begun_near and 1 <= l <= cols)]
        group = int(ls[-1] > cols)
        value = product(
            [xt[:, at(l)] for l in ls] + [gt[:, at(l)] for l in outside] + [xe[group], ge[group]],
            [
                [factor_of(cvp, l, a, b) for l in ls]
                + [factor_of(ghp, l, a, b) for l in outside]
                + end_factors(cvp, group, a, b)
                + end_factors(ghp, group, a, b)
                for a, b in unit
            ],
        )
        for n, (a, b) in enumerate(unit):
            term = value[:, n * ch:(n + 1) * ch]
            sums[place(a, b), :] = sums[place(a, b), :] + term if begun_near else term

    for unit in units[:3]:
        terms_near(unit)
    g_near.wait_recv()
    when_outer(h_far.wait_recv)
    widen(as_f32(gr[...]), g3, 0)
    widen(as_f32(hf[...]), h3, cols + 2)
    bias_sum = jnp.zeros((1, ch), F32)
    for q in range(cols - 1):
        bias_sum = bias_sum + curve(q)
    backward(cols)
    flip(g3, 0, gt)
    flip(g3, cols + 1, gt)
    for n in range(2):
        flip_ends(g3, n, ge)
    bias_sum = bias_sum + curve(cols - 1)
    st[...] = jnp.zeros_like(st)
    st[0:1, :] = bias_sum
    st[1:2, :] = squares

    def halos_sent():
        for copy in (x_near, h_near, g_near):
            copy.wait_send()
        when_outer(*[copy.wait_send for copy in x_far + [up_far, h_far]])

    if not scatter:
        for unit in units:
            terms_rest(unit)
        stat_ref[...] = st[...]
        halos_sent()
    else:
        (pf, pr, pb, rb, zb, rz, own, og, qb, rq, qown, qc, sr, s2, sb, sz, pair_send, pair_recv, sc_send,
         sc_recv, z_send, z_recv, ag_send, ag_recv, q_send, q_recv, qc_send, qc_recv, stat_send,
         stat_recv) = scratch[32:]
        half = tiles // 2
        z = t // 2
        thick = clips * piece

        def clip_at(step):
            return lax.rem(k + step, clips)

        def z_at(step):
            return lax.rem(z + step, half)

        def block_at(tile, start, size):
            return pl.ds(pl.multiple_of(tile * block + start, 16), size)

        stat_pair = remote(st, sr, stat_send.at[0], stat_recv.at[0], (k, other))
        stat_clip = [
            remote(s2, sb.at[k], stat_send.at[dk], stat_recv.at[1 + k], (clip_at(dk), t))
            for dk in range(1, clips)
        ]
        stat_z = [
            remote(sb.at[k], sz.at[z], stat_send.at[clips + dz], stat_recv.at[1 + clips + z],
                   (k, 2 * z_at(dz) + core))
            for dz in range(1, half)
        ]

        def stats_a():
            stat_pair.wait_recv()
            s2[...] = st[...] + sr[...]
            for copy in stat_clip:
                copy.start()

        def stats_b():
            total = s2[...]
            for dk in range(1, clips):
                slot = clip_at(dk)
                remote(s2, sb.at[slot], stat_send.at[dk], stat_recv.at[1 + slot], (slot, t)).wait_recv()
                total = total + sb[slot]
            sb[k] = total
            for copy in stat_z:
                copy.start()

        def stats_c():
            total = sb[k]
            for dz in range(1, half):
                slot = z_at(dz)
                remote(
                    sb.at[k], sz.at[slot], stat_send.at[clips + dz], stat_recv.at[1 + clips + slot],
                    (k, 2 * slot + core),
                ).wait_recv()
                total = total + sz[slot]
            bias_out[...] = factor * total[0:1, :]
            pen_ref[...] = 0.5 * factor * jnp.sum(total[1:2, :], axis=1, keepdims=True)

        stat_pair.start()

        def ready(j):
            lo, hi = 2 * j * block, (2 * j + 2) * block
            return set(range(lo // wide, (hi - 1) // wide + 1))

        pairs = [
            remote(pf.at[block_at(2 * j + 1 - core, 0, block)], pr.at[j], pair_send.at[j], pair_recv.at[j],
                   (k, other))
            for j in range(half)
        ]
        clip_sends = [
            [
                remote(pb.at[j, clip_at(dk)], rb.at[j, k], sc_send.at[j, dk], sc_recv.at[j, k],
                       (clip_at(dk), t))
                for dk in range(1, clips)
            ]
            for j in range(half)
        ]
        z_sends = [
            remote(zb.at[j], rz.at[z], z_send.at[j], z_recv.at[z], (k, 2 * j + core)) for j in range(half)
        ]
        q_sends = [
            remote(qb.at[j], rq.at[z], q_send.at[j], q_recv.at[z], (k, 2 * j + core)) for j in range(half)
        ]

        def after_pair(j):
            pairs[j].wait_recv()
            second = pf[block_at(2 * j + core, thick, block - thick), :] + pr[j, thick:block]

            @pl.when(z == j)
            def _():
                qown[...] = second

            @pl.when(z != j)
            def _():
                qb[j] = second.astype(BF16)
                q_sends[j].start()
            first = pf[block_at(2 * j + core, 0, thick), :] + pr[j, 0:thick]
            pf[block_at(2 * j + core, 0, thick), :] = first
            pb[j] = first.astype(BF16).reshape(clips, piece, ch)
            for copy in clip_sends[j]:
                copy.start()

        def over_z(j):
            total = pf[block_at(2 * j + core, k * piece, piece), :]
            for dk in range(1, clips):
                slot = clip_at(dk)
                remote(pb.at[j, slot], rb.at[j, slot], sc_send.at[j, dk], sc_recv.at[j, slot],
                       (slot, t)).wait_recv()
                total = total + rb[j, slot].astype(F32)

            @pl.when(z == j)
            def _():
                own[...] = total

            @pl.when(z != j)
            def _():
                zb[j] = total.astype(BF16)
                z_sends[j].start()

        done, begun, paired = (set(), set()), [], []
        for n, part in enumerate((units[:3], units[3:])):
            for unit in part:
                terms_rest(unit)
                for a, b in unit:
                    done[0].add(3 * a + b)
                    done[1].add(3 * a + 2 - b)
            fresh = [j for j in range(half) if j not in begun and ready(j) <= done[0] & done[1]]
            for j in fresh:
                pairs[j].start()
            if n == 0:
                stats_a()
            for j in paired:
                after_pair(j)
            begun += fresh
            paired = fresh
        for j in paired:
            after_pair(j)
        stats_b()
        halos_sent()
        for copy in stat_clip + [stat_pair] + pairs:
            copy.wait_send()
        for j in begun:
            over_z(j)

        total = qown[...]
        for dz in range(1, half):
            slot = z_at(dz)
            remote(qb.at[0], rq.at[slot], q_send.at[0], q_recv.at[slot], (k, 2 * slot + core)).wait_recv()
            total = total + rq[slot].astype(F32)
        qc[k] = total.astype(BF16)
        spreads = [
            remote(qc.at[k], qc.at[k], qc_send.at[dk], qc_recv.at[k], (clip_at(dk), t))
            for dk in range(1, clips)
        ]
        for copy in spreads:
            copy.start()

        total = own[...]
        for dz in range(1, half):
            slot = z_at(dz)
            remote(zb.at[0], rz.at[slot], z_send.at[0], z_recv.at[slot], (k, 2 * slot + core)).wait_recv()
            total = total + rz[slot].astype(F32)
        og[k] = factor * total
        gathers = [
            remote(og.at[k], og.at[k], ag_send.at[dk], ag_recv.at[k], (clip_at(dk), t))
            for dk in range(1, clips)
        ]
        for copy in gathers:
            copy.start()
        stats_c()
        for j in range(half):
            for copy in clip_sends[j]:
                copy.wait_send()

            @pl.when(z != j)
            def _():
                z_sends[j].wait_send()
                q_sends[j].wait_send()
        for dk in range(1, clips):
            slot = clip_at(dk)
            remote(qc.at[slot], qc.at[slot], qc_send.at[dk], qc_recv.at[slot], (slot, t)).wait_recv()
        total = qc[0].astype(F32)
        for slot in range(1, clips):
            total = total + qc[slot].astype(F32)
        out_ref[thick:block, :] = factor * total
        for dk in range(1, clips):
            slot = clip_at(dk)
            remote(og.at[slot], og.at[slot], ag_send.at[dk], ag_recv.at[slot], (slot, t)).wait_recv()
        out_ref[0:thick, :] = og[...].reshape(thick, ch)
        for copy in gathers + spreads + stat_z:
            copy.wait_send()


def shards(clip_features, upstream, weight, conv_bias):
    count, frames, cols, rows, ch = clip_features.shape
    clips = lax.axis_size("clip")
    tiles = lax.axis_size("tile")
    factor = r1_weight / (count * clips * frames * rows * cols * tiles)
    weight_rows = weight.shape[0] * ch
    block = weight_rows // tiles
    scatter = block % 16 == 0
    piece = max(1, block * SHARE // (1600 * clips)) * 16
    wide = 3 * ch
    main = frames - frames % (128 // rows)
    ends = -(-(cols + 1) * (frames - main) * rows // 128) * 128
    geo = (clips, tiles, frames, cols, rows, ch, block, piece, scatter, factor)
    dma = pltpu.SemaphoreType.DMA

    def field(width):
        return pltpu.VMEM((width, frames + 1, rows, wide), BF16)

    flipped = pltpu.VMEM((wide, (cols + 2) * main * rows), BF16)
    flipped_ends = pltpu.VMEM((2, wide, ends), BF16)
    thin = pltpu.VMEM((cols, frames + 2, rows, ch), BF16)
    pair, single = pltpu.VMEM((10 * ch, 2 * ch), BF16), pltpu.VMEM((8 * ch, ch), BF16)
    edge = pltpu.VMEM((frames, rows, ch), BF16)
    scratch = [
        pltpu.VMEM((frames * rows, ch), F32),
        pltpu.VMEM((frames * rows, ch), F32),
        pltpu.VMEM((1, ch), F32),
        pltpu.VMEM((cols + 3, frames, rows, ch), BF16),
        pltpu.VMEM((cols + 1, frames, rows, ch), BF16),
        pair, single, pair, single,
        field(cols + 3), field(cols + 3), field(cols + 2), flipped, flipped, flipped_ends, flipped_ends,
        thin, thin,
        pltpu.VMEM((cols, frames * rows, ch), F32),
        edge, edge, edge, edge,
        pltpu.VMEM((8, ch), F32),
        dma, dma((cols,)), dma((cols,)), dma((10,)), dma((3,)), dma((3,)), dma((4,)), dma((4,)),
    ]
    half = tiles // 2
    out_rows = weight_rows
    if scatter:
        out_rows = block
        others = block - clips * piece
        scratch += [
            pltpu.VMEM((weight_rows, ch), F32),
            pltpu.VMEM((half, block, ch), F32),
            pltpu.VMEM((half, clips, piece, ch), BF16),
            pltpu.VMEM((half, clips, piece, ch), BF16),
            pltpu.VMEM((half, piece, ch), BF16),
            pltpu.VMEM((half, piece, ch), BF16),
            pltpu.VMEM((piece, ch), F32),
            pltpu.VMEM((clips, piece, ch), F32),
            pltpu.VMEM((half, others, ch), BF16),
            pltpu.VMEM((half, others, ch), BF16),
            pltpu.VMEM((others, ch), F32),
            pltpu.VMEM((clips, others, ch), BF16),
            pltpu.VMEM((8, ch), F32),
            pltpu.VMEM((8, ch), F32),
            pltpu.VMEM((clips, 8, ch), F32),
            pltpu.VMEM((half, 8, ch), F32),
            dma((half,)), dma((half,)), dma((half, clips)), dma((half, clips)),
            dma((half,)), dma((half,)), dma((clips,)), dma((clips,)),
            dma((half,)), dma((half,)), dma((clips,)), dma((clips,)),
            dma((clips + half,)), dma((1 + clips + half,)),
        ]
    hbm = pl.BlockSpec(memory_space=pltpu.HBM)
    vmem = pl.BlockSpec(memory_space=pltpu.VMEM)
    outs = (jax.ShapeDtypeStruct((out_rows, ch), F32), jax.ShapeDtypeStruct((8, ch), F32))
    if scatter:
        outs = (pltpu.VMEM((out_rows, ch), F32), pltpu.VMEM((1, ch), F32), jax.ShapeDtypeStruct((1, 1), F32))
    results = pl.pallas_call(
        functools.partial(kernel, geo),
        out_shape=outs,
        in_specs=[hbm, hbm, hbm, hbm],
        out_specs=(vmem,) * len(outs),
        scratch_shapes=scratch,
        compiler_params=pltpu.CompilerParams(
            collective_id=0, has_side_effects=True, vmem_limit_bytes=60 * 1024 * 1024
        ),
        name="r1_section",
    )(
        clip_features.reshape(frames, cols, rows, ch),
        upstream.reshape(frames, cols, rows, ch),
        weight.reshape(9, wide, ch),
        conv_bias.reshape(1, ch),
    )
    if scatter:
        return results[0], results[1].reshape(ch), results[2].reshape(())
    grads, stats = results
    grads = factor * lax.psum(lax.psum_scatter(grads, "tile", scatter_dimension=0, tiled=True), "clip")
    stats = lax.psum(stats, ("clip", "tile"))
    return grads, factor * stats[0], 0.5 * factor * jnp.sum(stats[1])


def solution(mesh):
    in_specs = (P("clip", None, "tile", None, None), P("clip", None, "tile", None, None), P(), P())
    out_specs = (P("tile", None), P(), P())
    return jax.shard_map(shards, mesh=mesh, in_specs=in_specs, out_specs=out_specs, check_vma=False)
```

```python
import functools

import jax
import jax.numpy as jnp
from jax import lax
from jax.experimental import pallas as pl
from jax.experimental.pallas import tpu as pltpu
from jax.sharding import PartitionSpec as P

r1_weight = 10.0
MESH = pl.DeviceIdType.MESH
BF16 = jnp.bfloat16
F32 = jnp.float32
SHARE = 75


def kernel(geo, x_hbm, up_hbm, w_hbm, bias_hbm, out_ref, *rest):
    (clips, tiles, frames, cols, rows, ch, block, piece, scatter, factor) = geo
    if scatter:
        bias_out, pen_ref, *scratch = rest
    else:
        stat_ref, *scratch = rest
    (kept_x, kept_h, bias_ref, xb, upb, wv, ww, wt, wu, x3, h3, g3, xt, gt, xe, ge, ghp, cvp, sig, hr, hf, gs, gr, st,
     bias_sem, load_sem, up_sem, w_sem, near_send, near_recv, far_send, far_recv) = scratch[:32]
    k = lax.axis_index("clip")
    t = lax.axis_index("tile")
    core = lax.rem(t, 2)
    other = t + 1 - 2 * core
    outer = t - 1 + 2 * core
    has_outer = jnp.logical_and(outer >= 0, outer < tiles)
    outer_at = (k, jnp.clip(outer, 0, tiles - 1))
    cells = frames * rows
    wide = 3 * ch
    last = 9 * ch - ch
    main = xt.shape[1] // ((cols + 2) * rows)
    lanes = main * rows

    def column_at(q):
        return cols - 1 - q + core * (2 * q - cols + 1)

    def tap_at(b):
        return 2 - b + core * (2 * b - 2)

    peers = [(0, dt) for dt in (1, tiles - 1)] + [(dk, 0) for dk in range(1, clips)]
    peers += [(0, dt) for dt in range(2, tiles - 1)]
    barrier = pltpu.get_barrier_semaphore()
    if scatter:
        for dk, dt in peers:
            pl.semaphore_signal(
                barrier, inc=1,
                device_id=(lax.rem(k + dk, clips), lax.rem(t + dt, tiles)), device_id_type=MESH,
            )
    else:
        for step in (1, tiles - 1):
            pl.semaphore_signal(
                barrier, inc=1, device_id=(k, lax.rem(t + step, tiles)), device_id_type=MESH
            )

    x_loads = [
        pltpu.make_async_copy(x_hbm.at[:, column_at(q)], xb.at[q + 1], load_sem.at[q]) for q in range(cols)
    ]
    for copy in x_loads:
        copy.start()
    w_loads = [
        pltpu.make_async_copy(
            w_hbm.at[3 * a + tap_at(b)], wv.at[wide * b:wide * (b + 1), a * ch:(a + 1) * ch],
            w_sem.at[3 * a + b],
        )
        for a in range(2)
        for b in range(3)
    ]
    w_loads += [
        pltpu.make_async_copy(w_hbm.at[6 + tap_at(b)], ww.at[wide * b:wide * (b + 1)], w_sem.at[6 + b])
        for b in range(2)
    ]
    w_loads += [
        pltpu.make_async_copy(w_hbm.at[6 + tap_at(2), 0:2 * ch], ww.at[2 * wide:last], w_sem.at[8]),
        pltpu.make_async_copy(
            w_hbm.at[6 + tap_at(2), 2 * ch:wide], wv.at[3 * wide:3 * wide + ch, ch:2 * ch], w_sem.at[9]
        ),
    ]
    for copy in w_loads:
        copy.start()
    up_loads = [
        pltpu.make_async_copy(up_hbm.at[:, column_at(q)], upb.at[q], up_sem.at[q]) for q in range(cols)
    ]
    for copy in up_loads:
        copy.start()
    bias_load = pltpu.make_async_copy(bias_hbm, bias_ref, bias_sem)
    bias_load.start()

    def remote(src, dst, send_sem, recv_sem, device):
        return pltpu.make_async_remote_copy(
            src_ref=src, dst_ref=dst, send_sem=send_sem, recv_sem=recv_sem,
            device_id=device, device_id_type=MESH,
        )

    def to_other(n, src, dst):
        return remote(src, dst, near_send.at[n], near_recv.at[n], (k, other))

    def to_outer(n, src, dst):
        return remote(src, dst, far_send.at[n], far_recv.at[n], outer_at)

    x_near = to_other(0, xb.at[1], xb.at[0])
    h_near = to_other(1, ghp.at[0, 1:frames + 1], hr)
    g_near = to_other(2, gs, gr)
    x_far = [to_outer(i, xb.at[cols - i], xb.at[cols + 1 + i]) for i in range(2)]
    up_far = to_outer(2, up_hbm.at[:, column_at(cols - 1)], upb.at[cols])
    h_far = to_outer(3, ghp.at[cols - 2, 1:frames + 1], hf)

    def when_outer(*steps):
        @pl.when(has_outer)
        def _():
            for step in steps:
                step()

    if scatter:
        pl.semaphore_wait(barrier, len(peers))
    else:
        pl.semaphore_wait(barrier, 2)
    for copy in x_loads:
        copy.wait()
    x_near.start()
    when_outer(x_far[0].start, x_far[1].start, up_far.start)

    zero_wide = jnp.zeros((rows, wide), BF16)
    for field in (x3, h3, g3):
        for w in range(field.shape[0]):
            field[w, frames] = zero_wide
    zero_thin = jnp.zeros((rows, ch), BF16)
    for field in (ghp, cvp):
        for w in range(cols):
            for f in (0, frames + 1):
                field[w, f] = zero_thin
    for field in (wv, wt):
        field[3 * wide:, 0:ch] = jnp.zeros((ch, ch), BF16)
    zero_col = jnp.zeros((frames, rows, ch), BF16)

    @pl.when(jnp.logical_not(has_outer))
    def _():
        for i in range(2):
            xb[cols + 1 + i] = zero_col
        upb[cols] = zero_col
        hf[...] = zero_col

    row_at = lax.rem(lax.broadcasted_iota(jnp.int32, (cells, ch), 0), rows)
    first_row = row_at == 0
    last_row = row_at == rows - 1

    def widen(value, field, w):
        before = jnp.where(first_row, 0.0, pltpu.roll(value, 1, 0)).astype(BF16)
        after = jnp.where(last_row, 0.0, pltpu.roll(value, cells - 1, 0)).astype(BF16)
        shape = (frames, rows, ch)
        field[w, 0:frames, :, 0:ch] = before.reshape(shape)
        field[w, 0:frames, :, ch:2 * ch] = value.astype(BF16).reshape(shape)
        field[w, 0:frames, :, 2 * ch:] = after.reshape(shape)

    def flip(field, w, target):
        target[:, w * lanes:(w + 1) * lanes] = field[w, 0:main].reshape(lanes, wide).T

    spare = frames - main
    ends = (cols + 1) * spare * rows

    def flip_ends(field, n, target):
        parts = [field[w + n, main:frames].reshape(spare * rows, wide) for w in range(cols + 1)]
        if target.shape[2] > ends:
            parts.append(jnp.zeros((target.shape[2] - ends, wide), BF16))
        target[n] = jnp.concatenate(parts, axis=0).T

    def shifted(both, third):
        edge = jnp.zeros((rows, ch), F32)
        before = jnp.concatenate([edge, both[0:cells - rows, 0:ch]], axis=0)
        after = jnp.concatenate([third[rows:], edge], axis=0)
        return both[:, ch:] + before + after

    def across(field, q, lo, hi):
        return [field[q + b, 0:frames].reshape(cells, wide) for b in range(lo, hi)]

    def ahead(field, q):
        return field[q + 2, 1:frames + 1, :, 2 * ch:].reshape(cells, ch)

    def conv(field, pair, single, q):
        left = jnp.concatenate(across(field, q, 0, 3) + [ahead(field, q)], axis=1)
        both = jnp.dot(left, pair[...], preferred_element_type=F32)
        third = jnp.dot(left[:, 0:last], single[...], preferred_element_type=F32)
        return shifted(both, third)

    def conv_early(field, pair, single, q, kept):
        left = jnp.concatenate(across(field, q, 0, 2), axis=1)
        both = jnp.dot(left, pair[0:2 * wide], preferred_element_type=F32)
        third = jnp.dot(left, single[0:2 * wide], preferred_element_type=F32)
        kept[...] = shifted(both, third)

    def conv_late(field, pair, single, q, kept):
        left = jnp.concatenate(across(field, q, 2, 3) + [ahead(field, q)], axis=1)
        both = jnp.dot(left, pair[2 * wide:], preferred_element_type=F32)
        third = jnp.dot(left[:, 0:last - 2 * wide], single[2 * wide:], preferred_element_type=F32)
        return kept[...] + shifted(both, third)

    def as_f32(column):
        return column.reshape(cells, ch).astype(F32)

    def forward(q, kept=None):
        hidden = (conv_late(x3, wv, ww, q, kept) if kept is not None else conv(x3, wv, ww, q)) + bias_ref[...]
        if q == cols:
            when_outer(up_far.wait_recv)
        sigma = jax.nn.sigmoid(hidden)
        value = (as_f32(upb[q]) * (0.2 + 0.8 * sigma)).astype(BF16)
        if q < cols:
            sig[q] = sigma
            ghp[q, 1:frames + 1] = value.reshape(frames, rows, ch)
        widen(value.astype(F32), h3, q + 1)

    def backward(q, kept=None):
        value = conv_late(h3, wt, wu, q, kept) if kept is not None else conv(h3, wt, wu, q)
        if q == cols:
            value = jnp.where(has_outer, value, 0.0)
        if q == 0:
            gs[...] = value.astype(BF16).reshape(frames, rows, ch)
        widen(value.astype(BF16).astype(F32), g3, q + 1)
        return jnp.sum(value * value, axis=0, keepdims=True)

    def curve(q):
        sigma = sig[q]
        value = (conv(g3, wv, ww, q) * as_f32(upb[q]) * (0.8 * sigma * (1.0 - sigma))).astype(BF16)
        cvp[q, 1:frames + 1] = value.reshape(frames, rows, ch)
        return jnp.sum(value.astype(F32), axis=0, keepdims=True)

    for q in range(cols):
        widen(as_f32(xb[q + 1]), x3, q + 1)
    for copy in w_loads + up_loads + [bias_load]:
        copy.wait()
    inner = list(range(1, cols - 1))
    for q in inner:
        forward(q)
    when_outer(h_far.start)
    for a in range(3):
        for b in range(3):
            for c in range(3):
                row = wide * (2 - b) + ch * (2 - c)
                if a == 0 and row == last:
                    block_of = wv[3 * wide:, ch:2 * ch]
                elif a == 0:
                    block_of = ww[row:row + ch, :]
                else:
                    block_of = wv[row:row + ch, ch * (2 - a):ch * (3 - a)]
                row = wide * b + ch * c
                if a == 2 and row == last:
                    wt[3 * wide:, ch:2 * ch] = block_of.T
                elif a == 2:
                    wu[row:row + ch, :] = block_of.T
                else:
                    wt[row:row + ch, ch * a:ch * (a + 1)] = block_of.T
    conv_early(x3, wv, ww, cols - 1, kept_x)
    x_near.wait_recv()
    widen(as_f32(xb[0]), x3, 0)
    forward(0)
    h_near.start()
    for q in range(-1, cols):
        flip(x3, q + 1, xt)
    flip_ends(x3, 0, xe)
    conv_early(h3, wt, wu, cols - 2, kept_h)
    h_near.wait_recv()
    widen(as_f32(hr[...]), h3, 0)
    squares = backward(0)
    g_near.start()

    when_outer(x_far[0].wait_recv)
    widen(as_f32(xb[cols + 1]), x3, cols + 1)
    forward(cols - 1, kept_x)
    for q in inner:
        squares = squares + backward(q, kept_h if q == cols - 2 else None)
    flip(x3, cols + 1, xt)
    flip_ends(x3, 1, xe)
    when_outer(x_far[1].wait_recv)
    widen(as_f32(xb[cols + 2]), x3, cols + 2)
    forward(cols)
    squares = squares + backward(cols - 1)
    for q in range(cols):
        flip(g3, q + 1, gt)

    units = [((0, b), (2, b)) for b in range(3)] + [((1, 0), (1, 1)), ((1, 2),)]

    def factor_of(pads, l, a, b):
        if 0 <= l - b < cols:
            return pads[l - b, 2 - a:2 - a + main].reshape(lanes, ch)
        return jnp.zeros((lanes, ch), BF16)

    def end_factors(pads, n, a, b):
        parts = []
        for w in range(cols + 1):
            if 0 <= w + n - b < cols:
                parts.append(pads[w + n - b, 2 - a + main:2 - a + frames].reshape(spare * rows, ch))
            else:
                parts.append(jnp.zeros((spare * rows, ch), BF16))
        if xe.shape[2] > ends:
            parts.append(jnp.zeros((xe.shape[2] - ends, ch), BF16))
        return parts

    def columns_of(unit):
        return sorted({w + b for _, b in unit for w in range(cols)})

    sums = scratch[32] if scatter else out_ref

    def place(a, b):
        return pl.ds(pl.multiple_of(wide * (3 * a + tap_at(b)), ch), wide)

    def at(l):
        return slice(l * lanes, (l + 1) * lanes)

    def product(left, right):
        left = jnp.concatenate(left, axis=1)
        right = jnp.concatenate([jnp.concatenate(parts, axis=0) for parts in right], axis=1)
        return jnp.dot(left, right, preferred_element_type=F32)

    def terms_near(unit):
        inside = [l for l in columns_of(unit) if 1 <= l <= cols]
        value = product(
            [gt[:, at(l)] for l in inside],
            [[factor_of(ghp, l, a, b) for l in inside] for a, b in unit],
        )
        for n, (a, b) in enumerate(unit):
            sums[place(a, b), :] = value[:, n * ch:(n + 1) * ch]

    def terms_rest(unit):
        ls = columns_of(unit)
        begun_near = unit in units[:3]
        outside = [l for l in ls if not (begun_near and 1 <= l <= cols)]
        group = int(ls[-1] > cols)
        value = product(
            [xt[:, at(l)] for l in ls] + [gt[:, at(l)] for l in outside] + [xe[group], ge[group]],
            [
                [factor_of(cvp, l, a, b) for l in ls]
                + [factor_of(ghp, l, a, b) for l in outside]
                + end_factors(cvp, group, a, b)
                + end_factors(ghp, group, a, b)
                for a, b in unit
            ],
        )
        for n, (a, b) in enumerate(unit):
            term = value[:, n * ch:(n + 1) * ch]
            sums[place(a, b), :] = sums[place(a, b), :] + term if begun_near else term

    for unit in units[:3]:
        terms_near(unit)
    g_near.wait_recv()
    when_outer(h_far.wait_recv)
    widen(as_f32(gr[...]), g3, 0)
    widen(as_f32(hf[...]), h3, cols + 2)
    bias_sum = jnp.zeros((1, ch), F32)
    for q in range(cols - 1):
        bias_sum = bias_sum + curve(q)
    backward(cols)
    flip(g3, 0, gt)
    flip(g3, cols + 1, gt)
    for n in range(2):
        flip_ends(g3, n, ge)
    bias_sum = bias_sum + curve(cols - 1)
    st[...] = jnp.zeros_like(st)
    st[0:1, :] = bias_sum
    st[1:2, :] = squares

    def halos_sent():
        for copy in (x_near, h_near, g_near):
            copy.wait_send()
        when_outer(*[copy.wait_send for copy in x_far + [up_far, h_far]])

    if not scatter:
        for unit in units:
            terms_rest(unit)
        stat_ref[...] = st[...]
        halos_sent()
    else:
        (pf, pr, pb, rb, zb, rz, own, og, qb, rq, qown, qc, sr, s2, sb, sz, pair_send, pair_recv, sc_send,
         sc_recv, z_send, z_recv, ag_send, ag_recv, q_send, q_recv, qc_send, qc_recv, stat_send,
         stat_recv) = scratch[32:]
        half = tiles // 2
        z = t // 2
        thick = clips * piece

        def clip_at(step):
            return lax.rem(k + step, clips)

        def z_at(step):
            return lax.rem(z + step, half)

        def block_at(tile, start, size):
            return pl.ds(pl.multiple_of(tile * block + start, 16), size)

        stat_pair = remote(st, sr, stat_send.at[0], stat_recv.at[0], (k, other))
        stat_clip = [
            remote(s2, sb.at[k], stat_send.at[dk], stat_recv.at[1 + k], (clip_at(dk), t))
            for dk in range(1, clips)
        ]
        stat_z = [
            remote(sb.at[k], sz.at[z], stat_send.at[clips + dz], stat_recv.at[1 + clips + z],
                   (k, 2 * z_at(dz) + core))
            for dz in range(1, half)
        ]

        def stats_a():
            stat_pair.wait_recv()
            s2[...] = st[...] + sr[...]
            for copy in stat_clip:
                copy.start()

        def stats_b():
            total = s2[...]
            for dk in range(1, clips):
                slot = clip_at(dk)
                remote(s2, sb.at[slot], stat_send.at[dk], stat_recv.at[1 + slot], (slot, t)).wait_recv()
                total = total + sb[slot]
            sb[k] = total
            for copy in stat_z:
                copy.start()

        def stats_c():
            total = sb[k]
            for dz in range(1, half):
                slot = z_at(dz)
                remote(
                    sb.at[k], sz.at[slot], stat_send.at[clips + dz], stat_recv.at[1 + clips + slot],
                    (k, 2 * slot + core),
                ).wait_recv()
                total = total + sz[slot]
            bias_out[...] = factor * total[0:1, :]
            pen_ref[...] = 0.5 * factor * jnp.sum(total[1:2, :], axis=1, keepdims=True)

        stat_pair.start()

        def ready(j):
            lo, hi = 2 * j * block, (2 * j + 2) * block
            return set(range(lo // wide, (hi - 1) // wide + 1))

        pairs = [
            remote(pf.at[block_at(2 * j + 1 - core, 0, block)], pr.at[j], pair_send.at[j], pair_recv.at[j],
                   (k, other))
            for j in range(half)
        ]
        clip_sends = [
            [
                remote(pb.at[j, clip_at(dk)], rb.at[j, k], sc_send.at[j, dk], sc_recv.at[j, k],
                       (clip_at(dk), t))
                for dk in range(1, clips)
            ]
            for j in range(half)
        ]
        z_sends = [
            remote(zb.at[j], rz.at[z], z_send.at[j], z_recv.at[z], (k, 2 * j + core)) for j in range(half)
        ]
        q_sends = [
            remote(qb.at[j], rq.at[z], q_send.at[j], q_recv.at[z], (k, 2 * j + core)) for j in range(half)
        ]

        def after_pair(j):
            pairs[j].wait_recv()
            second = pf[block_at(2 * j + core, thick, block - thick), :] + pr[j, thick:block]

            @pl.when(z == j)
            def _():
                qown[...] = second

            @pl.when(z != j)
            def _():
                qb[j] = second.astype(BF16)
                q_sends[j].start()
            first = pf[block_at(2 * j + core, 0, thick), :] + pr[j, 0:thick]
            pf[block_at(2 * j + core, 0, thick), :] = first
            pb[j] = first.astype(BF16).reshape(clips, piece, ch)
            for copy in clip_sends[j]:
                copy.start()

        def over_z(j):
            total = pf[block_at(2 * j + core, k * piece, piece), :]
            for dk in range(1, clips):
                slot = clip_at(dk)
                remote(pb.at[j, slot], rb.at[j, slot], sc_send.at[j, dk], sc_recv.at[j, slot],
                       (slot, t)).wait_recv()
                total = total + rb[j, slot].astype(F32)

            @pl.when(z == j)
            def _():
                own[...] = total

            @pl.when(z != j)
            def _():
                zb[j] = total.astype(BF16)
                z_sends[j].start()

        done, begun, paired = (set(), set()), [], []
        for n, part in enumerate((units[:3], units[3:])):
            for unit in part:
                terms_rest(unit)
                for a, b in unit:
                    done[0].add(3 * a + b)
                    done[1].add(3 * a + 2 - b)
            fresh = [j for j in range(half) if j not in begun and ready(j) <= done[0] & done[1]]
            for j in fresh:
                pairs[j].start()
            if n == 1:
                stats_a()
            for j in paired:
                after_pair(j)
            begun += fresh
            paired = fresh
        for j in paired:
            after_pair(j)
        stats_b()
        halos_sent()
        for copy in stat_clip + [stat_pair] + pairs:
            copy.wait_send()
        for j in begun:
            over_z(j)

        total = qown[...]
        for dz in range(1, half):
            slot = z_at(dz)
            remote(qb.at[0], rq.at[slot], q_send.at[0], q_recv.at[slot], (k, 2 * slot + core)).wait_recv()
            total = total + rq[slot].astype(F32)
        qc[k] = total.astype(BF16)
        spreads = [
            remote(qc.at[k], qc.at[k], qc_send.at[dk], qc_recv.at[k], (clip_at(dk), t))
            for dk in range(1, clips)
        ]
        for copy in spreads:
            copy.start()

        total = own[...]
        for dz in range(1, half):
            slot = z_at(dz)
            remote(zb.at[0], rz.at[slot], z_send.at[0], z_recv.at[slot], (k, 2 * slot + core)).wait_recv()
            total = total + rz[slot].astype(F32)
        og[k] = factor * total
        gathers = [
            remote(og.at[k], og.at[k], ag_send.at[dk], ag_recv.at[k], (clip_at(dk), t))
            for dk in range(1, clips)
        ]
        for copy in gathers:
            copy.start()
        stats_c()
        for j in range(half):
            for copy in clip_sends[j]:
                copy.wait_send()

            @pl.when(z != j)
            def _():
                z_sends[j].wait_send()
                q_sends[j].wait_send()
        for dk in range(1, clips):
            slot = clip_at(dk)
            remote(qc.at[slot], qc.at[slot], qc_send.at[dk], qc_recv.at[slot], (slot, t)).wait_recv()
        total = qc[0].astype(F32)
        for slot in range(1, clips):
            total = total + qc[slot].astype(F32)
        out_ref[thick:block, :] = factor * total
        for dk in range(1, clips):
            slot = clip_at(dk)
            remote(og.at[slot], og.at[slot], ag_send.at[dk], ag_recv.at[slot], (slot, t)).wait_recv()
        out_ref[0:thick, :] = og[...].reshape(thick, ch)
        for copy in gathers + spreads + stat_z:
            copy.wait_send()


def shards(clip_features, upstream, weight, conv_bias):
    count, frames, cols, rows, ch = clip_features.shape
    clips = lax.axis_size("clip")
    tiles = lax.axis_size("tile")
    factor = r1_weight / (count * clips * frames * rows * cols * tiles)
    weight_rows = weight.shape[0] * ch
    block = weight_rows // tiles
    scatter = block % 16 == 0
    piece = max(1, block * SHARE // (1600 * clips)) * 16
    wide = 3 * ch
    main = frames - frames % (128 // rows)
    ends = -(-(cols + 1) * (frames - main) * rows // 128) * 128
    geo = (clips, tiles, frames, cols, rows, ch, block, piece, scatter, factor)
    dma = pltpu.SemaphoreType.DMA

    def field(width):
        return pltpu.VMEM((width, frames + 1, rows, wide), BF16)

    flipped = pltpu.VMEM((wide, (cols + 2) * main * rows), BF16)
    flipped_ends = pltpu.VMEM((2, wide, ends), BF16)
    thin = pltpu.VMEM((cols, frames + 2, rows, ch), BF16)
    pair, single = pltpu.VMEM((10 * ch, 2 * ch), BF16), pltpu.VMEM((8 * ch, ch), BF16)
    edge = pltpu.VMEM((frames, rows, ch), BF16)
    scratch = [
        pltpu.VMEM((frames * rows, ch), F32),
        pltpu.VMEM((frames * rows, ch), F32),
        pltpu.VMEM((1, ch), F32),
        pltpu.VMEM((cols + 3, frames, rows, ch), BF16),
        pltpu.VMEM((cols + 1, frames, rows, ch), BF16),
        pair, single, pair, single,
        field(cols + 3), field(cols + 3), field(cols + 2), flipped, flipped, flipped_ends, flipped_ends,
        thin, thin,
        pltpu.VMEM((cols, frames * rows, ch), F32),
        edge, edge, edge, edge,
        pltpu.VMEM((8, ch), F32),
        dma, dma((cols,)), dma((cols,)), dma((10,)), dma((3,)), dma((3,)), dma((4,)), dma((4,)),
    ]
    half = tiles // 2
    out_rows = weight_rows
    if scatter:
        out_rows = block
        others = block - clips * piece
        scratch += [
            pltpu.VMEM((weight_rows, ch), F32),
            pltpu.VMEM((half, block, ch), F32),
            pltpu.VMEM((half, clips, piece, ch), BF16),
            pltpu.VMEM((half, clips, piece, ch), BF16),
            pltpu.VMEM((half, piece, ch), BF16),
            pltpu.VMEM((half, piece, ch), BF16),
            pltpu.VMEM((piece, ch), F32),
            pltpu.VMEM((clips, piece, ch), F32),
            pltpu.VMEM((half, others, ch), BF16),
            pltpu.VMEM((half, others, ch), BF16),
            pltpu.VMEM((others, ch), F32),
            pltpu.VMEM((clips, others, ch), BF16),
            pltpu.VMEM((8, ch), F32),
            pltpu.VMEM((8, ch), F32),
            pltpu.VMEM((clips, 8, ch), F32),
            pltpu.VMEM((half, 8, ch), F32),
            dma((half,)), dma((half,)), dma((half, clips)), dma((half, clips)),
            dma((half,)), dma((half,)), dma((clips,)), dma((clips,)),
            dma((half,)), dma((half,)), dma((clips,)), dma((clips,)),
            dma((clips + half,)), dma((1 + clips + half,)),
        ]
    hbm = pl.BlockSpec(memory_space=pltpu.HBM)
    vmem = pl.BlockSpec(memory_space=pltpu.VMEM)
    outs = (jax.ShapeDtypeStruct((out_rows, ch), F32), jax.ShapeDtypeStruct((8, ch), F32))
    if scatter:
        outs = (pltpu.VMEM((out_rows, ch), F32), pltpu.VMEM((1, ch), F32), jax.ShapeDtypeStruct((1, 1), F32))
    results = pl.pallas_call(
        functools.partial(kernel, geo),
        out_shape=outs,
        in_specs=[hbm, hbm, hbm, hbm],
        out_specs=(vmem,) * len(outs),
        scratch_shapes=scratch,
        compiler_params=pltpu.CompilerParams(
            collective_id=0, has_side_effects=True, vmem_limit_bytes=60 * 1024 * 1024
        ),
        name="r1_section",
    )(
        clip_features.reshape(frames, cols, rows, ch),
        upstream.reshape(frames, cols, rows, ch),
        weight.reshape(9, wide, ch),
        conv_bias.reshape(1, ch),
    )
    if scatter:
        return results[0], results[1].reshape(ch), results[2].reshape(())
    grads, stats = results
    grads = factor * lax.psum(lax.psum_scatter(grads, "tile", scatter_dimension=0, tiled=True), "clip")
    stats = lax.psum(stats, ("clip", "tile"))
    return grads, factor * stats[0], 0.5 * factor * jnp.sum(stats[1])


def solution(mesh):
    in_specs = (P("clip", None, "tile", None, None), P("clip", None, "tile", None, None), P(), P())
    out_specs = (P("tile", None), P(), P())
    return jax.shard_map(shards, mesh=mesh, in_specs=in_specs, out_specs=out_specs, check_vma=False)
```

```python
import functools

import jax
import jax.numpy as jnp
from jax import lax
from jax.experimental import pallas as pl
from jax.experimental.pallas import tpu as pltpu
from jax.sharding import PartitionSpec as P

r1_weight = 10.0
MESH = pl.DeviceIdType.MESH
BF16 = jnp.bfloat16
F32 = jnp.float32
SHARE = 75


def kernel(geo, x_hbm, up_hbm, w_hbm, bias_hbm, out_ref, *rest):
    (clips, tiles, frames, cols, rows, ch, block, piece, scatter, factor) = geo
    if scatter:
        bias_out, pen_ref, *scratch = rest
    else:
        stat_ref, *scratch = rest
    (kept_x, kept_h, bias_ref, xb, upb, wv, ww, wt, wu, x3, h3, g3, xt, gt, xe, ge, ghp, cvp, sig, hr, hf, gs, gr, st,
     bias_sem, load_sem, up_sem, w_sem, near_send, near_recv, far_send, far_recv) = scratch[:32]
    k = lax.axis_index("clip")
    t = lax.axis_index("tile")
    core = lax.rem(t, 2)
    other = t + 1 - 2 * core
    outer = t - 1 + 2 * core
    has_outer = jnp.logical_and(outer >= 0, outer < tiles)
    outer_at = (k, jnp.clip(outer, 0, tiles - 1))
    cells = frames * rows
    wide = 3 * ch
    last = 9 * ch - ch
    main = xt.shape[1] // ((cols + 2) * rows)
    lanes = main * rows

    def column_at(q):
        return cols - 1 - q + core * (2 * q - cols + 1)

    def tap_at(b):
        return 2 - b + core * (2 * b - 2)

    peers = [(0, dt) for dt in (1, tiles - 1)] + [(dk, 0) for dk in range(1, clips)]
    peers += [(0, dt) for dt in range(2, tiles - 1)]
    barrier = pltpu.get_barrier_semaphore()
    if scatter:
        for dk, dt in peers:
            pl.semaphore_signal(
                barrier, inc=1,
                device_id=(lax.rem(k + dk, clips), lax.rem(t + dt, tiles)), device_id_type=MESH,
            )
    else:
        for step in (1, tiles - 1):
            pl.semaphore_signal(
                barrier, inc=1, device_id=(k, lax.rem(t + step, tiles)), device_id_type=MESH
            )

    x_loads = [
        pltpu.make_async_copy(x_hbm.at[:, column_at(q)], xb.at[q + 1], load_sem.at[q]) for q in range(cols)
    ]
    for copy in x_loads:
        copy.start()
    w_loads = [
        pltpu.make_async_copy(
            w_hbm.at[3 * a + tap_at(b)], wv.at[wide * b:wide * (b + 1), a * ch:(a + 1) * ch],
            w_sem.at[3 * a + b],
        )
        for a in range(2)
        for b in range(3)
    ]
    w_loads += [
        pltpu.make_async_copy(w_hbm.at[6 + tap_at(b)], ww.at[wide * b:wide * (b + 1)], w_sem.at[6 + b])
        for b in range(2)
    ]
    w_loads += [
        pltpu.make_async_copy(w_hbm.at[6 + tap_at(2), 0:2 * ch], ww.at[2 * wide:last], w_sem.at[8]),
        pltpu.make_async_copy(
            w_hbm.at[6 + tap_at(2), 2 * ch:wide], wv.at[3 * wide:3 * wide + ch, ch:2 * ch], w_sem.at[9]
        ),
    ]
    for copy in w_loads:
        copy.start()
    up_loads = [
        pltpu.make_async_copy(up_hbm.at[:, column_at(q)], upb.at[q], up_sem.at[q]) for q in range(cols)
    ]
    for copy in up_loads:
        copy.start()
    bias_load = pltpu.make_async_copy(bias_hbm, bias_ref, bias_sem)
    bias_load.start()

    def remote(src, dst, send_sem, recv_sem, device):
        return pltpu.make_async_remote_copy(
            src_ref=src, dst_ref=dst, send_sem=send_sem, recv_sem=recv_sem,
            device_id=device, device_id_type=MESH,
        )

    def to_other(n, src, dst):
        return remote(src, dst, near_send.at[n], near_recv.at[n], (k, other))

    def to_outer(n, src, dst):
        return remote(src, dst, far_send.at[n], far_recv.at[n], outer_at)

    x_near = to_other(0, xb.at[1], xb.at[0])
    h_near = to_other(1, ghp.at[0, 1:frames + 1], hr)
    g_near = to_other(2, gs, gr)
    x_far = [to_outer(i, xb.at[cols - i], xb.at[cols + 1 + i]) for i in range(2)]
    up_far = to_outer(2, up_hbm.at[:, column_at(cols - 1)], upb.at[cols])
    h_far = to_outer(3, ghp.at[cols - 2, 1:frames + 1], hf)

    def when_outer(*steps):
        @pl.when(has_outer)
        def _():
            for step in steps:
                step()

    if scatter:
        pl.semaphore_wait(barrier, len(peers))
    else:
        pl.semaphore_wait(barrier, 2)
    for copy in x_loads:
        copy.wait()
    x_near.start()
    when_outer(x_far[0].start, x_far[1].start, up_far.start)

    zero_wide = jnp.zeros((rows, wide), BF16)
    for field in (x3, h3, g3):
        for w in range(field.shape[0]):
            field[w, frames] = zero_wide
    zero_thin = jnp.zeros((rows, ch), BF16)
    for field in (ghp, cvp):
        for w in range(cols):
            for f in (0, frames + 1):
                field[w, f] = zero_thin
    for field in (wv, wt):
        field[3 * wide:, 0:ch] = jnp.zeros((ch, ch), BF16)
    zero_col = jnp.zeros((frames, rows, ch), BF16)

    @pl.when(jnp.logical_not(has_outer))
    def _():
        for i in range(2):
            xb[cols + 1 + i] = zero_col
        upb[cols] = zero_col
        hf[...] = zero_col

    row_at = lax.rem(lax.broadcasted_iota(jnp.int32, (cells, ch), 0), rows)
    first_row = row_at == 0
    last_row = row_at == rows - 1

    def widen(value, field, w):
        before = jnp.where(first_row, 0.0, pltpu.roll(value, 1, 0)).astype(BF16)
        after = jnp.where(last_row, 0.0, pltpu.roll(value, cells - 1, 0)).astype(BF16)
        shape = (frames, rows, ch)
        field[w, 0:frames, :, 0:ch] = before.reshape(shape)
        field[w, 0:frames, :, ch:2 * ch] = value.astype(BF16).reshape(shape)
        field[w, 0:frames, :, 2 * ch:] = after.reshape(shape)

    def flip(field, w, target):
        target[:, w * lanes:(w + 1) * lanes] = field[w, 0:main].reshape(lanes, wide).T

    spare = frames - main
    ends = (cols + 1) * spare * rows

    def flip_ends(field, n, target):
        parts = [field[w + n, main:frames].reshape(spare * rows, wide) for w in range(cols + 1)]
        if target.shape[2] > ends:
            parts.append(jnp.zeros((target.shape[2] - ends, wide), BF16))
        target[n] = jnp.concatenate(parts, axis=0).T

    def shifted(both, third):
        edge = jnp.zeros((rows, ch), F32)
        before = jnp.concatenate([edge, both[0:cells - rows, 0:ch]], axis=0)
        after = jnp.concatenate([third[rows:], edge], axis=0)
        return both[:, ch:] + before + after

    def across(field, q, lo, hi):
        return [field[q + b, 0:frames].reshape(cells, wide) for b in range(lo, hi)]

    def ahead(field, q):
        return field[q + 2, 1:frames + 1, :, 2 * ch:].reshape(cells, ch)

    def conv(field, pair, single, q):
        left = jnp.concatenate(across(field, q, 0, 3) + [ahead(field, q)], axis=1)
        both = jnp.dot(left, pair[...], preferred_element_type=F32)
        third = jnp.dot(left[:, 0:last], single[...], preferred_element_type=F32)
        return shifted(both, third)

    def conv_early(field, pair, single, q, kept):
        left = jnp.concatenate(across(field, q, 0, 2), axis=1)
        both = jnp.dot(left, pair[0:2 * wide], preferred_element_type=F32)
        third = jnp.dot(left, single[0:2 * wide], preferred_element_type=F32)
        kept[...] = shifted(both, third)

    def conv_late(field, pair, single, q, kept):
        left = jnp.concatenate(across(field, q, 2, 3) + [ahead(field, q)], axis=1)
        both = jnp.dot(left, pair[2 * wide:], preferred_element_type=F32)
        third = jnp.dot(left[:, 0:last - 2 * wide], single[2 * wide:], preferred_element_type=F32)
        return kept[...] + shifted(both, third)

    def as_f32(column):
        return column.reshape(cells, ch).astype(F32)

    def forward(q, kept=None):
        hidden = (conv_late(x3, wv, ww, q, kept) if kept is not None else conv(x3, wv, ww, q)) + bias_ref[...]
        if q == cols:
            when_outer(up_far.wait_recv)
        sigma = jax.nn.sigmoid(hidden)
        value = (as_f32(upb[q]) * (0.2 + 0.8 * sigma)).astype(BF16)
        if q < cols:
            sig[q] = sigma
            ghp[q, 1:frames + 1] = value.reshape(frames, rows, ch)
        widen(value.astype(F32), h3, q + 1)

    def backward(q, kept=None):
        value = conv_late(h3, wt, wu, q, kept) if kept is not None else conv(h3, wt, wu, q)
        if q == cols:
            value = jnp.where(has_outer, value, 0.0)
        if q == 0:
            gs[...] = value.astype(BF16).reshape(frames, rows, ch)
        widen(value.astype(BF16).astype(F32), g3, q + 1)
        return jnp.sum(value * value, axis=0, keepdims=True)

    def curve(q):
        sigma = sig[q]
        value = (conv(g3, wv, ww, q) * as_f32(upb[q]) * (0.8 * sigma * (1.0 - sigma))).astype(BF16)
        cvp[q, 1:frames + 1] = value.reshape(frames, rows, ch)
        return jnp.sum(value.astype(F32), axis=0, keepdims=True)

    for q in range(cols):
        widen(as_f32(xb[q + 1]), x3, q + 1)
    for copy in w_loads + up_loads + [bias_load]:
        copy.wait()
    inner = list(range(1, cols - 1))
    for q in inner:
        forward(q)
    when_outer(h_far.start)
    for a in range(3):
        for b in range(3):
            for c in range(3):
                row = wide * (2 - b) + ch * (2 - c)
                if a == 0 and row == last:
                    block_of = wv[3 * wide:, ch:2 * ch]
                elif a == 0:
                    block_of = ww[row:row + ch, :]
                else:
                    block_of = wv[row:row + ch, ch * (2 - a):ch * (3 - a)]
                row = wide * b + ch * c
                if a == 2 and row == last:
                    wt[3 * wide:, ch:2 * ch] = block_of.T
                elif a == 2:
                    wu[row:row + ch, :] = block_of.T
                else:
                    wt[row:row + ch, ch * a:ch * (a + 1)] = block_of.T
    conv_early(x3, wv, ww, cols - 1, kept_x)
    x_near.wait_recv()
    widen(as_f32(xb[0]), x3, 0)
    forward(0)
    h_near.start()
    for q in range(-1, cols):
        flip(x3, q + 1, xt)
    flip_ends(x3, 0, xe)
    h_near.wait_recv()
    widen(as_f32(hr[...]), h3, 0)
    squares = backward(0)
    g_near.start()

    when_outer(x_far[0].wait_recv)
    widen(as_f32(xb[cols + 1]), x3, cols + 1)
    forward(cols - 1, kept_x)
    for q in inner:
        squares = squares + backward(q)
    flip(x3, cols + 1, xt)
    flip_ends(x3, 1, xe)
    when_outer(x_far[1].wait_recv)
    widen(as_f32(xb[cols + 2]), x3, cols + 2)
    forward(cols)
    squares = squares + backward(cols - 1)
    for q in range(cols):
        flip(g3, q + 1, gt)

    units = [((0, b), (2, b)) for b in range(3)] + [((1, 0), (1, 1)), ((1, 2),)]

    def factor_of(pads, l, a, b):
        if 0 <= l - b < cols:
            return pads[l - b, 2 - a:2 - a + main].reshape(lanes, ch)
        return jnp.zeros((lanes, ch), BF16)

    def end_factors(pads, n, a, b):
        parts = []
        for w in range(cols + 1):
            if 0 <= w + n - b < cols:
                parts.append(pads[w + n - b, 2 - a + main:2 - a + frames].reshape(spare * rows, ch))
            else:
                parts.append(jnp.zeros((spare * rows, ch), BF16))
        if xe.shape[2] > ends:
            parts.append(jnp.zeros((xe.shape[2] - ends, ch), BF16))
        return parts

    def columns_of(unit):
        return sorted({w + b for _, b in unit for w in range(cols)})

    sums = scratch[32] if scatter else out_ref

    def place(a, b):
        return pl.ds(pl.multiple_of(wide * (3 * a + tap_at(b)), ch), wide)

    def at(l):
        return slice(l * lanes, (l + 1) * lanes)

    def product(left, right):
        left = jnp.concatenate(left, axis=1)
        right = jnp.concatenate([jnp.concatenate(parts, axis=0) for parts in right], axis=1)
        return jnp.dot(left, right, preferred_element_type=F32)

    def terms_near(unit):
        inside = [l for l in columns_of(unit) if 1 <= l <= cols]
        value = product(
            [gt[:, at(l)] for l in inside],
            [[factor_of(ghp, l, a, b) for l in inside] for a, b in unit],
        )
        for n, (a, b) in enumerate(unit):
            sums[place(a, b), :] = value[:, n * ch:(n + 1) * ch]

    def terms_rest(unit):
        ls = columns_of(unit)
        begun_near = unit in units[:3]
        outside = [l for l in ls if not (begun_near and 1 <= l <= cols)]
        group = int(ls[-1] > cols)
        value = product(
            [xt[:, at(l)] for l in ls] + [gt[:, at(l)] for l in outside] + [xe[group], ge[group]],
            [
                [factor_of(cvp, l, a, b) for l in ls]
                + [factor_of(ghp, l, a, b) for l in outside]
                + end_factors(cvp, group, a, b)
                + end_factors(ghp, group, a, b)
                for a, b in unit
            ],
        )
        for n, (a, b) in enumerate(unit):
            term = value[:, n * ch:(n + 1) * ch]
            sums[place(a, b), :] = sums[place(a, b), :] + term if begun_near else term

    for unit in units[:3]:
        terms_near(unit)
    g_near.wait_recv()
    when_outer(h_far.wait_recv)
    widen(as_f32(gr[...]), g3, 0)
    widen(as_f32(hf[...]), h3, cols + 2)
    bias_sum = jnp.zeros((1, ch), F32)
    for q in range(cols - 1):
        bias_sum = bias_sum + curve(q)
    backward(cols)
    flip(g3, 0, gt)
    flip(g3, cols + 1, gt)
    for n in range(2):
        flip_ends(g3, n, ge)
    bias_sum = bias_sum + curve(cols - 1)
    st[...] = jnp.zeros_like(st)
    st[0:1, :] = bias_sum
    st[1:2, :] = squares

    def halos_sent():
        for copy in (x_near, h_near, g_near):
            copy.wait_send()
        when_outer(*[copy.wait_send for copy in x_far + [up_far, h_far]])

    if not scatter:
        for unit in units:
            terms_rest(unit)
        stat_ref[...] = st[...]
        halos_sent()
    else:
        (pf, pr, pb, rb, zb, rz, own, og, qb, rq, qown, qc, sr, s2, sb, sz, pair_send, pair_recv, sc_send,
         sc_recv, z_send, z_recv, ag_send, ag_recv, q_send, q_recv, qc_send, qc_recv, stat_send,
         stat_recv) = scratch[32:]
        half = tiles // 2
        z = t // 2
        thick = clips * piece

        def clip_at(step):
            return lax.rem(k + step, clips)

        def z_at(step):
            return lax.rem(z + step, half)

        def block_at(tile, start, size):
            return pl.ds(pl.multiple_of(tile * block + start, 16), size)

        stat_pair = remote(st, sr, stat_send.at[0], stat_recv.at[0], (k, other))
        stat_clip = [
            remote(s2, sb.at[k], stat_send.at[dk], stat_recv.at[1 + k], (clip_at(dk), t))
            for dk in range(1, clips)
        ]
        stat_z = [
            remote(sb.at[k], sz.at[z], stat_send.at[clips + dz], stat_recv.at[1 + clips + z],
                   (k, 2 * z_at(dz) + core))
            for dz in range(1, half)
        ]

        def stats_a():
            stat_pair.wait_recv()
            s2[...] = st[...] + sr[...]
            for copy in stat_clip:
                copy.start()

        def stats_b():
            total = s2[...]
            for dk in range(1, clips):
                slot = clip_at(dk)
                remote(s2, sb.at[slot], stat_send.at[dk], stat_recv.at[1 + slot], (slot, t)).wait_recv()
                total = total + sb[slot]
            sb[k] = total
            for copy in stat_z:
                copy.start()

        def stats_c():
            total = sb[k]
            for dz in range(1, half):
                slot = z_at(dz)
                remote(
                    sb.at[k], sz.at[slot], stat_send.at[clips + dz], stat_recv.at[1 + clips + slot],
                    (k, 2 * slot + core),
                ).wait_recv()
                total = total + sz[slot]
            bias_out[...] = factor * total[0:1, :]
            pen_ref[...] = 0.5 * factor * jnp.sum(total[1:2, :], axis=1, keepdims=True)

        stat_pair.start()

        def ready(j):
            lo, hi = 2 * j * block, (2 * j + 2) * block
            return set(range(lo // wide, (hi - 1) // wide + 1))

        pairs = [
            remote(pf.at[block_at(2 * j + 1 - core, 0, block)], pr.at[j], pair_send.at[j], pair_recv.at[j],
                   (k, other))
            for j in range(half)
        ]
        clip_sends = [
            [
                remote(pb.at[j, clip_at(dk)], rb.at[j, k], sc_send.at[j, dk], sc_recv.at[j, k],
                       (clip_at(dk), t))
                for dk in range(1, clips)
            ]
            for j in range(half)
        ]
        z_sends = [
            remote(zb.at[j], rz.at[z], z_send.at[j], z_recv.at[z], (k, 2 * j + core)) for j in range(half)
        ]
        q_sends = [
            remote(qb.at[j], rq.at[z], q_send.at[j], q_recv.at[z], (k, 2 * j + core)) for j in range(half)
        ]

        def after_pair(j):
            pairs[j].wait_recv()
            second = pf[block_at(2 * j + core, thick, block - thick), :] + pr[j, thick:block]

            @pl.when(z == j)
            def _():
                qown[...] = second

            @pl.when(z != j)
            def _():
                qb[j] = second.astype(BF16)
                q_sends[j].start()
            first = pf[block_at(2 * j + core, 0, thick), :] + pr[j, 0:thick]
            pf[block_at(2 * j + core, 0, thick), :] = first
            pb[j] = first.astype(BF16).reshape(clips, piece, ch)
            for copy in clip_sends[j]:
                copy.start()

        def over_z(j):
            total = pf[block_at(2 * j + core, k * piece, piece), :]
            for dk in range(1, clips):
                slot = clip_at(dk)
                remote(pb.at[j, slot], rb.at[j, slot], sc_send.at[j, dk], sc_recv.at[j, slot],
                       (slot, t)).wait_recv()
                total = total + rb[j, slot].astype(F32)

            @pl.when(z == j)
            def _():
                own[...] = total

            @pl.when(z != j)
            def _():
                zb[j] = total.astype(BF16)
                z_sends[j].start()

        done, begun, paired = (set(), set()), [], []
        for n, part in enumerate((units[:3], units[3:])):
            for unit in part:
                terms_rest(unit)
                for a, b in unit:
                    done[0].add(3 * a + b)
                    done[1].add(3 * a + 2 - b)
            fresh = [j for j in range(half) if j not in begun and ready(j) <= done[0] & done[1]]
            for j in fresh:
                pairs[j].start()
            if n == 1:
                stats_a()
            for j in paired:
                after_pair(j)
            begun += fresh
            paired = fresh
        for j in paired:
            after_pair(j)
        stats_b()
        halos_sent()
        for copy in stat_clip + [stat_pair] + pairs:
            copy.wait_send()
        for j in begun:
            over_z(j)

        total = qown[...]
        for dz in range(1, half):
            slot = z_at(dz)
            remote(qb.at[0], rq.at[slot], q_send.at[0], q_recv.at[slot], (k, 2 * slot + core)).wait_recv()
            total = total + rq[slot].astype(F32)
        qc[k] = total.astype(BF16)
        spreads = [
            remote(qc.at[k], qc.at[k], qc_send.at[dk], qc_recv.at[k], (clip_at(dk), t))
            for dk in range(1, clips)
        ]
        for copy in spreads:
            copy.start()

        total = own[...]
        for dz in range(1, half):
            slot = z_at(dz)
            remote(zb.at[0], rz.at[slot], z_send.at[0], z_recv.at[slot], (k, 2 * slot + core)).wait_recv()
            total = total + rz[slot].astype(F32)
        og[k] = factor * total
        gathers = [
            remote(og.at[k], og.at[k], ag_send.at[dk], ag_recv.at[k], (clip_at(dk), t))
            for dk in range(1, clips)
        ]
        for copy in gathers:
            copy.start()
        stats_c()
        for j in range(half):
            for copy in clip_sends[j]:
                copy.wait_send()

            @pl.when(z != j)
            def _():
                z_sends[j].wait_send()
                q_sends[j].wait_send()
        for dk in range(1, clips):
            slot = clip_at(dk)
            remote(qc.at[slot], qc.at[slot], qc_send.at[dk], qc_recv.at[slot], (slot, t)).wait_recv()
        total = qc[0].astype(F32)
        for slot in range(1, clips):
            total = total + qc[slot].astype(F32)
        out_ref[thick:block, :] = factor * total
        for dk in range(1, clips):
            slot = clip_at(dk)
            remote(og.at[slot], og.at[slot], ag_send.at[dk], ag_recv.at[slot], (slot, t)).wait_recv()
        out_ref[0:thick, :] = og[...].reshape(thick, ch)
        for copy in gathers + spreads + stat_z:
            copy.wait_send()


def shards(clip_features, upstream, weight, conv_bias):
    count, frames, cols, rows, ch = clip_features.shape
    clips = lax.axis_size("clip")
    tiles = lax.axis_size("tile")
    factor = r1_weight / (count * clips * frames * rows * cols * tiles)
    weight_rows = weight.shape[0] * ch
    block = weight_rows // tiles
    scatter = block % 16 == 0
    piece = max(1, block * SHARE // (1600 * clips)) * 16
    wide = 3 * ch
    main = frames - frames % (128 // rows)
    ends = -(-(cols + 1) * (frames - main) * rows // 128) * 128
    geo = (clips, tiles, frames, cols, rows, ch, block, piece, scatter, factor)
    dma = pltpu.SemaphoreType.DMA

    def field(width):
        return pltpu.VMEM((width, frames + 1, rows, wide), BF16)

    flipped = pltpu.VMEM((wide, (cols + 2) * main * rows), BF16)
    flipped_ends = pltpu.VMEM((2, wide, ends), BF16)
    thin = pltpu.VMEM((cols, frames + 2, rows, ch), BF16)
    pair, single = pltpu.VMEM((10 * ch, 2 * ch), BF16), pltpu.VMEM((8 * ch, ch), BF16)
    edge = pltpu.VMEM((frames, rows, ch), BF16)
    scratch = [
        pltpu.VMEM((frames * rows, ch), F32),
        pltpu.VMEM((frames * rows, ch), F32),
        pltpu.VMEM((1, ch), F32),
        pltpu.VMEM((cols + 3, frames, rows, ch), BF16),
        pltpu.VMEM((cols + 1, frames, rows, ch), BF16),
        pair, single, pair, single,
        field(cols + 3), field(cols + 3), field(cols + 2), flipped, flipped, flipped_ends, flipped_ends,
        thin, thin,
        pltpu.VMEM((cols, frames * rows, ch), F32),
        edge, edge, edge, edge,
        pltpu.VMEM((8, ch), F32),
        dma, dma((cols,)), dma((cols,)), dma((10,)), dma((3,)), dma((3,)), dma((4,)), dma((4,)),
    ]
    half = tiles // 2
    out_rows = weight_rows
    if scatter:
        out_rows = block
        others = block - clips * piece
        scratch += [
            pltpu.VMEM((weight_rows, ch), F32),
            pltpu.VMEM((half, block, ch), F32),
            pltpu.VMEM((half, clips, piece, ch), BF16),
            pltpu.VMEM((half, clips, piece, ch), BF16),
            pltpu.VMEM((half, piece, ch), BF16),
            pltpu.VMEM((half, piece, ch), BF16),
            pltpu.VMEM((piece, ch), F32),
            pltpu.VMEM((clips, piece, ch), F32),
            pltpu.VMEM((half, others, ch), BF16),
            pltpu.VMEM((half, others, ch), BF16),
            pltpu.VMEM((others, ch), F32),
            pltpu.VMEM((clips, others, ch), BF16),
            pltpu.VMEM((8, ch), F32),
            pltpu.VMEM((8, ch), F32),
            pltpu.VMEM((clips, 8, ch), F32),
            pltpu.VMEM((half, 8, ch), F32),
            dma((half,)), dma((half,)), dma((half, clips)), dma((half, clips)),
            dma((half,)), dma((half,)), dma((clips,)), dma((clips,)),
            dma((half,)), dma((half,)), dma((clips,)), dma((clips,)),
            dma((clips + half,)), dma((1 + clips + half,)),
        ]
    hbm = pl.BlockSpec(memory_space=pltpu.HBM)
    vmem = pl.BlockSpec(memory_space=pltpu.VMEM)
    outs = (jax.ShapeDtypeStruct((out_rows, ch), F32), jax.ShapeDtypeStruct((8, ch), F32))
    if scatter:
        outs = (pltpu.VMEM((out_rows, ch), F32), pltpu.VMEM((1, ch), F32), jax.ShapeDtypeStruct((1, 1), F32))
    results = pl.pallas_call(
        functools.partial(kernel, geo),
        out_shape=outs,
        in_specs=[hbm, hbm, hbm, hbm],
        out_specs=(vmem,) * len(outs),
        scratch_shapes=scratch,
        compiler_params=pltpu.CompilerParams(
            collective_id=0, has_side_effects=True, vmem_limit_bytes=60 * 1024 * 1024
        ),
        name="r1_section",
    )(
        clip_features.reshape(frames, cols, rows, ch),
        upstream.reshape(frames, cols, rows, ch),
        weight.reshape(9, wide, ch),
        conv_bias.reshape(1, ch),
    )
    if scatter:
        return results[0], results[1].reshape(ch), results[2].reshape(())
    grads, stats = results
    grads = factor * lax.psum(lax.psum_scatter(grads, "tile", scatter_dimension=0, tiled=True), "clip")
    stats = lax.psum(stats, ("clip", "tile"))
    return grads, factor * stats[0], 0.5 * factor * jnp.sum(stats[1])


def solution(mesh):
    in_specs = (P("clip", None, "tile", None, None), P("clip", None, "tile", None, None), P(), P())
    out_specs = (P("tile", None), P(), P())
    return jax.shard_map(shards, mesh=mesh, in_specs=in_specs, out_specs=out_specs, check_vma=False)
```
